128 devices in a mesh: row: 16 (over z, x_hi, core), col: 8 (over x_lo, y).
Axes of the slice: x: 4 (x_hi: 2, x_lo: 2; x = x_hi * 2 + x_lo), y: 4, z: 4, core: 2. Of those that a mesh axis runs over, the one named last changes fastest.
Arguments:
- stored: bfloat16 [1024, 51200], P(('row', 'col')), may hold values from -24 to 24
- integrals: bfloat16 [51200, 25600], P('row', 'col'), may hold values from -0.02734375 to 0.02734375
- layout: int32 [1024], replicated, may hold values from 0 to 1023, each once
- partner: int32 [1024], replicated, may hold values from 0 to 1023, as said below
Outputs:
- residual_out: bfloat16 [1024, 25600], P('row', 'col')
The draws below stay inside these ranges and needn't reach their ends.
Inputs may be any that keep to these rules, and one draw needn't show every extreme that they name: partner is an involution without fixed points: partner[p] != p and partner[partner[p]] = p. `layout`: each slab pair stands in exactly one stored row.
All inputs are finite; a program needn't handle non-finite values.
Results may differ from the reference program's by a relative error of at most 0.001.
Values may be sent and summed in bfloat16 or wider, within the bound.
A program may use at most 128 MiB of HBM per device.

```python
import jax
import jax.numpy as jnp
from jax import lax

NV = 1600
AW = 16
P_SIZE = 1024
K = 51200
N = 25600


def draw_partner(key, part):
    order = jax.random.permutation(key, jnp.arange(P_SIZE, dtype=jnp.int32))
    firsts = order[0::2]
    seconds = order[1::2]
    coupled = jnp.zeros((P_SIZE,), jnp.int32).at[firsts].set(seconds)
    return coupled.at[seconds].set(firsts)


def spiked(result, key, source, target, shards_of, factor):
    owner, partner = [(jnp.arange(result.shape[dim]) // (result.shape[dim] // shards_of)).reshape([-1 if axis == dim else 1 for axis in range(result.ndim)]) for dim in (source, target)]
    chosen = jax.random.permutation(key, shards_of)[partner]
    strong = (owner == chosen) | (owner == (partner + shards_of // 2) % shards_of)
    return jnp.where(strong, factor * result, result)


def levels(stream_key, dims, shards, smallest, top_value):
    def one(axis_at, blocks):
        steps = jax.random.uniform(jax.random.fold_in(jax.random.fold_in(stream_key, 6), axis_at), (blocks,), jnp.float32, smallest / len(shards), top_value / len(shards))
        return jnp.repeat(jnp.exp(steps), dims[axis_at] // blocks).reshape((-1,) + (1,) * (len(dims) - axis_at - 1))

    gain = one(*shards[0])
    for cut in shards[1:]:
        gain = gain * one(*cut)
    return gain


def noise(own_key, dims, deviation, bound, cuts=(), kind=jnp.bfloat16):
    result = deviation * jax.random.normal(own_key, dims, jnp.float32)
    if cuts:
        result = result * levels(own_key, dims, cuts, -0.22, 0.18)
    return jnp.clip(result, -bound, bound).astype(kind)


def bell_draw_with(stream_key, dims, deviation, most, split, heavy, kind=jnp.bfloat16):
    result = deviation * jax.random.normal(stream_key, dims, jnp.float32)
    if split:
        result = result * levels(stream_key, dims, split, -0.22, 0.18)
    return jnp.clip(spiked(result, jax.random.fold_in(stream_key, 3), *heavy), -most, most).astype(kind)


def setup_inputs(seed: int = 0) -> dict:
    streams_of = jax.random.split(jax.random.key(seed), 5)
    stored = bell_draw_with(streams_of[0], (P_SIZE, K), 1.0, 24.0, ((0, 128),), (1, 0, 128, 5.5))
    integrals = noise(streams_of[1], (K, N), K ** -0.5, 0.02734375, ((0, 16), (1, 8)))
    layout = jax.random.permutation(streams_of[2], P_SIZE).astype(jnp.int32)
    partner = draw_partner(jax.random.fold_in(streams_of[4], 71), 0)
    return dict(stored=stored, integrals=integrals, layout=layout, partner=partner)


def reference(stored, integrals, layout, partner):
    amplitudes = jnp.zeros_like(stored).at[layout].set(stored)

    def one_block(block_index):
        columns = lax.dynamic_slice_in_dim(integrals, block_index * NV, NV, 1)
        return jnp.dot(amplitudes, columns, preferred_element_type=jnp.float32)

    blocks = lax.map(one_block, jnp.arange(AW, dtype=jnp.int32))
    ladder = jnp.transpose(blocks, (1, 0, 2)).reshape(P_SIZE, AW * NV)
    return (ladder - ladder[partner]).astype(jnp.bfloat16)
```

```python
import jax
import jax.numpy as jnp
from jax import lax
from jax.sharding import Mesh, PartitionSpec as P

ROW_AXES = ("z", "xh", "core")
COL_AXES = ("xl", "y")
N_CHUNKS = 5


def per_device(stored, integrals, layout, partner):
    local_rows = stored.shape[0]
    n_z = lax.axis_size("z")
    n_xh = lax.axis_size("xh")
    n_core = lax.axis_size("core")
    n_row = n_z * n_xh * n_core
    n_col = lax.axis_size("xl") * lax.axis_size("y")
    total = local_rows * n_row * n_col
    block = total // n_row

    regrouped = lax.all_to_all(stored, ROW_AXES, split_axis=1, concat_axis=0, tiled=True)
    gathered = lax.all_gather(regrouped, COL_AXES, axis=0, tiled=True)

    s = jnp.arange(total, dtype=jnp.int32)
    s_row = s // (local_rows * n_col)
    s_col = (s // local_rows) % n_col
    s_off = s % local_rows
    pos_of_stored = s_col * (n_row * local_rows) + s_row * local_rows + s_off
    inv = jnp.zeros((total,), jnp.int32).at[layout].set(s)

    i = jnp.arange(total, dtype=jnp.int32)
    t = i % block
    g = i // block
    xh = g % n_xh
    z = (g // n_xh) % n_z
    core = g // (n_xh * n_z)
    p_of_i = ((z * n_xh + xh) * n_core + core) * block + t
    pt = partner[p_of_i]
    pt_t = pt % block
    pt_g = pt // block
    pt_core = pt_g % n_core
    pt_xh = (pt_g // n_core) % n_xh
    pt_z = pt_g // (n_core * n_xh)
    partner_i = ((pt_core * n_z + pt_z) * n_xh + pt_xh) * block + pt_t

    amps = gathered[pos_of_stored[inv[p_of_i]]]

    n_cols = integrals.shape[1]
    width = n_cols // N_CHUNKS
    outs = []
    for j in range(N_CHUNKS):
        cols = integrals[:, j * width:(j + 1) * width]
        ladder = jnp.dot(amps, cols, preferred_element_type=jnp.float32)
        difference = ladder - ladder[partner_i]
        part = lax.psum_scatter(difference, "core", scatter_dimension=0, tiled=True)
        part = lax.psum_scatter(part, ("z", "xh"), scatter_dimension=0, tiled=True)
        outs.append(part.astype(jnp.bfloat16))
    return jnp.concatenate(outs, axis=1)


def solution(mesh):
    n_row, n_col = mesh.devices.shape
    fine = Mesh(mesh.devices.reshape(4, n_row // 8, 2, 2, n_col // 2), ROW_AXES + COL_AXES)
    return jax.shard_map(
        per_device,
        mesh=fine,
        in_specs=(P(ROW_AXES + COL_AXES, None), P(ROW_AXES, COL_AXES), P(), P()),
        out_specs=P(ROW_AXES, COL_AXES),
        check_vma=False,
    )
```

```python
import jax
import jax.numpy as jnp
from jax import lax
from jax.sharding import Mesh, PartitionSpec as P

ROW_AXES = ("z", "xh", "core")
COL_AXES = ("xl", "y")
N_CHUNKS = 4


def per_device(stored, integrals, layout, partner):
    local_rows = stored.shape[0]
    n_z = lax.axis_size("z")
    n_xh = lax.axis_size("xh")
    n_core = lax.axis_size("core")
    n_row = n_z * n_xh * n_core
    n_col = lax.axis_size("xl") * lax.axis_size("y")
    total = local_rows * n_row * n_col
    block = total // n_row

    regrouped = lax.all_to_all(stored, ROW_AXES, split_axis=1, concat_axis=0, tiled=True)
    gathered = lax.all_gather(regrouped, COL_AXES, axis=0, tiled=True)

    s = jnp.arange(total, dtype=jnp.int32)
    s_row = s // (local_rows * n_col)
    s_col = (s // local_rows) % n_col
    s_off = s % local_rows
    pos_of_stored = s_col * (n_row * local_rows) + s_row * local_rows + s_off
    inv = jnp.zeros((total,), jnp.int32).at[layout].set(s)

    amps = gathered[pos_of_stored[inv]]

    n_cols = integrals.shape[1]
    tiles = n_cols // 128
    bounds = [128 * (tiles * j // N_CHUNKS) for j in range(N_CHUNKS)] + [n_cols]
    outs = []
    for j in range(N_CHUNKS):
        cols = integrals[:, bounds[j]:bounds[j + 1]]
        ladder = jnp.dot(amps, cols, preferred_element_type=jnp.float32)
        difference = ladder - ladder[partner]
        part = lax.psum_scatter(difference, ROW_AXES, scatter_dimension=0, tiled=True)
        outs.append(part.astype(jnp.bfloat16))
    return jnp.concatenate(outs, axis=1)


def solution(mesh):
    n_row, n_col = mesh.devices.shape
    fine = Mesh(mesh.devices.reshape(4, n_row // 8, 2, 2, n_col // 2), ROW_AXES + COL_AXES)
    return jax.shard_map(
        per_device,
        mesh=fine,
        in_specs=(P(ROW_AXES + COL_AXES, None), P(ROW_AXES, COL_AXES), P(), P()),
        out_specs=P(ROW_AXES, COL_AXES),
        check_vma=False,
    )
```

```python
import jax
import jax.numpy as jnp
from jax import lax
from jax.sharding import Mesh, PartitionSpec as P

ROW_AXES = ("z", "xh", "core")
COL_AXES = ("xl", "y")


def per_device(stored, integrals, layout, partner):
    local_rows, k_total = stored.shape
    n_row = lax.axis_size(ROW_AXES)
    n_col = lax.axis_size(COL_AXES)
    total = local_rows * n_row * n_col
    k_local = integrals.shape[0]

    pieces = stored.reshape(local_rows, n_row, k_local).transpose(1, 0, 2)
    outgoing = jnp.broadcast_to(pieces[:, None], (n_row, n_col, local_rows, k_local)).reshape(total, k_local)
    by_stored = lax.all_to_all(outgoing, ROW_AXES + COL_AXES, split_axis=0, concat_axis=0, tiled=True)

    inv = jnp.zeros((total,), jnp.int32).at[layout].set(jnp.arange(total, dtype=jnp.int32))
    amps = by_stored[inv]

    ladder = jnp.dot(amps, integrals, preferred_element_type=jnp.float32)
    difference = ladder - ladder[partner]
    blocks = difference.reshape(n_row, total // n_row, difference.shape[1])
    received = lax.all_to_all(blocks, ROW_AXES, split_axis=0, concat_axis=0, tiled=True)
    return jnp.sum(received, axis=0).astype(jnp.bfloat16)


def solution(mesh):
    n_row, n_col = mesh.devices.shape
    fine = Mesh(mesh.devices.reshape(4, n_row // 8, 2, 2, n_col // 2), ROW_AXES + COL_AXES)
    return jax.shard_map(
        per_device,
        mesh=fine,
        in_specs=(P(ROW_AXES + COL_AXES, None), P(ROW_AXES, COL_AXES), P(), P()),
        out_specs=P(ROW_AXES, COL_AXES),
        check_vma=False,
    )
```

```python
import jax
import jax.numpy as jnp
from jax import lax
from jax.sharding import Mesh, PartitionSpec as P

ROW_AXES = ("z", "xh", "core")
COL_AXES = ("xl", "y")


def per_device(stored, integrals, layout, partner):
    local_rows = stored.shape[0]
    n_z = lax.axis_size("z")
    n_xh = lax.axis_size("xh")
    n_core = lax.axis_size("core")
    n_row = n_z * n_xh * n_core
    n_col = lax.axis_size(COL_AXES)
    total = local_rows * n_row * n_col
    block = total // n_row

    regrouped = lax.all_to_all(stored, ROW_AXES, split_axis=1, concat_axis=0, tiled=True)
    gathered = lax.all_gather(regrouped, COL_AXES, axis=0, tiled=True)

    s = jnp.arange(total, dtype=jnp.int32)
    s_row = s // (local_rows * n_col)
    s_col = (s // local_rows) % n_col
    s_off = s % local_rows
    pos_of_stored = s_col * (n_row * local_rows) + s_row * local_rows + s_off
    inv = jnp.zeros((total,), jnp.int32).at[layout].set(s)

    i = jnp.arange(total, dtype=jnp.int32)
    g = i // block
    xh = g % n_xh
    core = (g // n_xh) % n_core
    z = g // (n_xh * n_core)
    p_of_i = ((z * n_xh + xh) * n_core + core) * block + (i % block)
    q = partner[p_of_i]
    q_g = q // block
    q_core = q_g % n_core
    q_xh = (q_g // n_core) % n_xh
    q_z = q_g // (n_core * n_xh)
    partner_i = ((q_z * n_core + q_core) * n_xh + q_xh) * block + (q % block)

    amps = gathered[pos_of_stored[inv[p_of_i]]]
    ladder = jnp.dot(amps, integrals, preferred_element_type=jnp.float32)
    difference = ladder - ladder[partner_i]
    part = lax.psum_scatter(difference, ("z", "core"), scatter_dimension=0, tiled=True)
    part = lax.psum_scatter(part, "xh", scatter_dimension=0, tiled=True)
    return part.astype(jnp.bfloat16)


def solution(mesh):
    n_row, n_col = mesh.devices.shape
    fine = Mesh(mesh.devices.reshape(4, n_row // 8, 2, 2, n_col // 2), ROW_AXES + COL_AXES)
    return jax.shard_map(
        per_device,
        mesh=fine,
        in_specs=(P(ROW_AXES + COL_AXES, None), P(ROW_AXES, COL_AXES), P(), P()),
        out_specs=P(ROW_AXES, COL_AXES),
        check_vma=False,
    )
```

```python
import jax
import jax.numpy as jnp
from jax import lax
from jax.experimental import pallas as pl
from jax.experimental.pallas import tpu as pltpu
from jax.sharding import Mesh, PartitionSpec as P

ROW_AXES = ("z", "xh", "core")
COL_AXES = ("xl", "y")


def _antisym_kernel(idx_ref, own_ref, all_ref, out_ref, buf, sem):
    rows = out_ref.shape[0]
    base = pl.program_id(0) * rows

    def start(r, carry):
        src = idx_ref[base + r]
        pltpu.make_async_copy(all_ref.at[pl.ds(src, 1)], buf.at[pl.ds(r, 1)], sem.at[0]).start()
        return carry

    lax.fori_loop(0, rows, start, 0)
    pltpu.make_async_copy(all_ref.at[pl.ds(0, rows)], buf, sem.at[0]).wait()
    out_ref[...] = own_ref[...] - buf[...]


def antisymmetrize(ladder, partner_rows, rows=128):
    total, width = ladder.shape
    return pl.pallas_call(
        _antisym_kernel,
        grid_spec=pltpu.PrefetchScalarGridSpec(
            num_scalar_prefetch=1,
            grid=(total // rows,),
            in_specs=[
                pl.BlockSpec((rows, width), lambda b, idx: (b, 0)),
                pl.BlockSpec(memory_space=pl.ANY),
            ],
            out_specs=pl.BlockSpec((rows, width), lambda b, idx: (b, 0)),
            scratch_shapes=[pltpu.VMEM((rows, width), ladder.dtype), pltpu.SemaphoreType.DMA((1,))],
        ),
        out_shape=jax.ShapeDtypeStruct(ladder.shape, ladder.dtype),
        cost_estimate=pl.CostEstimate(flops=total * width, transcendentals=0, bytes_accessed=3 * total * width * 4),
    )(partner_rows, ladder, ladder)


def per_device(stored, integrals, layout, partner):
    local_rows = stored.shape[0]
    n_z = lax.axis_size("z")
    n_xh = lax.axis_size("xh")
    n_core = lax.axis_size("core")
    n_row = n_z * n_xh * n_core
    n_col = lax.axis_size(COL_AXES)
    total = local_rows * n_row * n_col
    block = total // n_row

    regrouped = lax.all_to_all(stored, ROW_AXES, split_axis=1, concat_axis=0, tiled=True)
    gathered = lax.all_gather(regrouped, COL_AXES, axis=0, tiled=True)

    s = jnp.arange(total, dtype=jnp.int32)
    s_row = s // (local_rows * n_col)
    s_col = (s // local_rows) % n_col
    s_off = s % local_rows
    pos_of_stored = s_col * (n_row * local_rows) + s_row * local_rows + s_off
    inv = jnp.zeros((total,), jnp.int32).at[layout].set(s)

    i = jnp.arange(total, dtype=jnp.int32)
    g = i // block
    xh = g % n_xh
    core = (g // n_xh) % n_core
    z = g // (n_xh * n_core)
    p_of_i = ((z * n_xh + xh) * n_core + core) * block + (i % block)
    q = partner[p_of_i]
    q_g = q // block
    q_core = q_g % n_core
    q_xh = (q_g // n_core) % n_xh
    q_z = q_g // (n_core * n_xh)
    partner_i = ((q_z * n_core + q_core) * n_xh + q_xh) * block + (q % block)

    amps = gathered[pos_of_stored[inv[p_of_i]]]
    ladder = jnp.dot(amps, integrals, preferred_element_type=jnp.float32)
    difference = antisymmetrize(ladder, partner_i)
    part = lax.psum_scatter(difference, ("z", "core"), scatter_dimension=0, tiled=True)
    part = lax.psum_scatter(part, "xh", scatter_dimension=0, tiled=True)
    return part.astype(jnp.bfloat16)


def solution(mesh):
    n_row, n_col = mesh.devices.shape
    fine = Mesh(mesh.devices.reshape(4, n_row // 8, 2, 2, n_col // 2), ROW_AXES + COL_AXES)
    return jax.shard_map(
        per_device,
        mesh=fine,
        in_specs=(P(ROW_AXES + COL_AXES, None), P(ROW_AXES, COL_AXES), P(), P()),
        out_specs=P(ROW_AXES, COL_AXES),
        check_vma=False,
    )
```

```python
import jax
import jax.numpy as jnp
from jax import lax
from jax.experimental import pallas as pl
from jax.experimental.pallas import tpu as pltpu
from jax.sharding import Mesh, PartitionSpec as P

ROW_AXES = ("z", "xh", "core")
COL_AXES = ("xl", "y")


def _antisym_kernel(own_idx, partner_idx, all_ref, out_ref, own_buf, partner_buf, sem):
    rows = out_ref.shape[0]
    step = pl.program_id(0)
    steps = pl.num_programs(0)

    def issue(at, slot):
        base = at * rows

        def body(r, carry):
            pltpu.make_async_copy(all_ref.at[pl.ds(own_idx[base + r], 1)], own_buf.at[slot, pl.ds(r, 1)], sem.at[0, slot]).start()
            pltpu.make_async_copy(all_ref.at[pl.ds(partner_idx[base + r], 1)], partner_buf.at[slot, pl.ds(r, 1)], sem.at[1, slot]).start()
            return carry

        lax.fori_loop(0, rows, body, 0)

    @pl.when(step == 0)
    def _():
        issue(0, 0)

    @pl.when(step + 1 < steps)
    def _():
        issue(step + 1, (step + 1) % 2)

    slot = step % 2
    pltpu.make_async_copy(all_ref.at[pl.ds(0, rows)], own_buf.at[slot], sem.at[0, slot]).wait()
    pltpu.make_async_copy(all_ref.at[pl.ds(0, rows)], partner_buf.at[slot], sem.at[1, slot]).wait()
    out_ref[...] = own_buf[slot] - partner_buf[slot]


def antisymmetrize(ladder, own_rows, partner_rows, rows=64):
    total, width = ladder.shape
    return pl.pallas_call(
        _antisym_kernel,
        grid_spec=pltpu.PrefetchScalarGridSpec(
            num_scalar_prefetch=2,
            grid=(total // rows,),
            in_specs=[pl.BlockSpec(memory_space=pl.ANY)],
            out_specs=pl.BlockSpec((rows, width), lambda b, own, other: (b, 0)),
            scratch_shapes=[
                pltpu.VMEM((2, rows, width), ladder.dtype),
                pltpu.VMEM((2, rows, width), ladder.dtype),
                pltpu.SemaphoreType.DMA((2, 2)),
            ],
        ),
        out_shape=jax.ShapeDtypeStruct(ladder.shape, ladder.dtype),
        compiler_params=pltpu.CompilerParams(dimension_semantics=("arbitrary",)),
        cost_estimate=pl.CostEstimate(flops=total * width, transcendentals=0, bytes_accessed=3 * total * width * 4),
    )(own_rows, partner_rows, ladder)


def per_device(stored, integrals, layout, partner):
    local_rows = stored.shape[0]
    n_z = lax.axis_size("z")
    n_xh = lax.axis_size("xh")
    n_core = lax.axis_size("core")
    n_row = n_z * n_xh * n_core
    n_col = lax.axis_size(COL_AXES)
    total = local_rows * n_row * n_col
    block = total // n_row

    regrouped = lax.all_to_all(stored, ROW_AXES, split_axis=1, concat_axis=0, tiled=True)
    gathered = lax.all_gather(regrouped, COL_AXES, axis=0, tiled=True)

    s = jnp.arange(total, dtype=jnp.int32)
    s_row = s // (local_rows * n_col)
    s_col = (s // local_rows) % n_col
    s_off = s % local_rows
    pos_of_stored = s_col * (n_row * local_rows) + s_row * local_rows + s_off
    inv = jnp.zeros((total,), jnp.int32).at[layout].set(s)

    i = jnp.arange(total, dtype=jnp.int32)
    g = i // block
    xh = g % n_xh
    core = (g // n_xh) % n_core
    z = g // (n_xh * n_core)
    p_of_i = ((z * n_xh + xh) * n_core + core) * block + (i % block)
    q = partner[p_of_i]

    ladder = jnp.dot(gathered, integrals, preferred_element_type=jnp.float32)
    difference = antisymmetrize(ladder, pos_of_stored[inv[p_of_i]], pos_of_stored[inv[q]])
    part = lax.psum_scatter(difference, ("z", "core"), scatter_dimension=0, tiled=True)
    part = lax.psum_scatter(part, "xh", scatter_dimension=0, tiled=True)
    return part.astype(jnp.bfloat16)


def solution(mesh):
    n_row, n_col = mesh.devices.shape
    fine = Mesh(mesh.devices.reshape(4, n_row // 8, 2, 2, n_col // 2), ROW_AXES + COL_AXES)
    return jax.shard_map(
        per_device,
        mesh=fine,
        in_specs=(P(ROW_AXES + COL_AXES, None), P(ROW_AXES, COL_AXES), P(), P()),
        out_specs=P(ROW_AXES, COL_AXES),
        check_vma=False,
    )
```

```python
import jax
import jax.numpy as jnp
from jax import lax
from jax.experimental import pallas as pl
from jax.experimental.pallas import tpu as pltpu
from jax.sharding import Mesh, PartitionSpec as P

ROW_AXES = ("z", "xh", "core")
COL_AXES = ("xl", "y")


def _antisym_kernel(own_idx, partner_idx, all_ref, out_ref, own_buf, partner_buf, sem):
    rows = out_ref.shape[0]
    step = pl.program_id(0)
    steps = pl.num_programs(0)

    def issue(at, slot):
        base = at * rows

        def body(r, carry):
            pltpu.make_async_copy(all_ref.at[pl.ds(own_idx[base + r], 1)], own_buf.at[slot, pl.ds(r, 1)], sem.at[0, slot]).start()
            pltpu.make_async_copy(all_ref.at[pl.ds(partner_idx[base + r], 1)], partner_buf.at[slot, pl.ds(r, 1)], sem.at[1, slot]).start()
            return carry

        lax.fori_loop(0, rows, body, 0)

    @pl.when(step == 0)
    def _():
        issue(0, 0)

    @pl.when(step + 1 < steps)
    def _():
        issue(step + 1, (step + 1) % 2)

    slot = step % 2
    pltpu.make_async_copy(all_ref.at[pl.ds(0, rows)], own_buf.at[slot], sem.at[0, slot]).wait()
    pltpu.make_async_copy(all_ref.at[pl.ds(0, rows)], partner_buf.at[slot], sem.at[1, slot]).wait()
    out_ref[...] = own_buf[slot] - partner_buf[slot]


def antisymmetrize(ladder, own_rows, partner_rows, rows=64):
    total, width = ladder.shape
    return pl.pallas_call(
        _antisym_kernel,
        grid_spec=pltpu.PrefetchScalarGridSpec(
            num_scalar_prefetch=2,
            grid=(total // rows,),
            in_specs=[pl.BlockSpec(memory_space=pl.ANY)],
            out_specs=pl.BlockSpec((rows, width), lambda b, own, other: (b, 0)),
            scratch_shapes=[
                pltpu.VMEM((2, rows, width), ladder.dtype),
                pltpu.VMEM((2, rows, width), ladder.dtype),
                pltpu.SemaphoreType.DMA((2, 2)),
            ],
        ),
        out_shape=jax.ShapeDtypeStruct(ladder.shape, ladder.dtype),
        compiler_params=pltpu.CompilerParams(dimension_semantics=("arbitrary",)),
        cost_estimate=pl.CostEstimate(flops=total * width, transcendentals=0, bytes_accessed=3 * total * width * 4),
    )(own_rows, partner_rows, ladder)


def _exchange_kernel(src_ref, out_ref, send_sem, recv_sem, local_sem):
    n_z, n_xh, n_core = (lax.axis_size(a) for a in ROW_AXES)
    n = n_z * n_xh * n_core
    z, xh, core, xl, y = (lax.axis_index(a) for a in ROW_AXES + COL_AXES)
    me = (z * n_xh + xh) * n_core + core

    def peer(k):
        t = lax.rem(me + k, n)
        return t, (t // (n_xh * n_core), lax.rem(t // n_core, n_xh), lax.rem(t, n_core), xl, y)

    barrier = pltpu.get_barrier_semaphore()
    for k in range(1, n):
        pl.semaphore_signal(barrier, inc=1, device_id=peer(k)[1], device_id_type=pl.DeviceIdType.MESH)
    pl.semaphore_wait(barrier, n - 1)

    local = pltpu.make_async_copy(src_ref.at[me], out_ref.at[me], local_sem.at[0])
    local.start()
    sends = []
    for k in range(1, n):
        t, where = peer(k)
        copy = pltpu.make_async_remote_copy(
            src_ref=src_ref.at[t],
            dst_ref=out_ref.at[me],
            send_sem=send_sem.at[k - 1],
            recv_sem=recv_sem.at[0],
            device_id=where,
            device_id_type=pl.DeviceIdType.MESH,
        )
        copy.start()
        sends.append(copy)
    for copy in sends:
        copy.wait_send()
    pltpu.make_async_copy(src_ref.at[pl.ds(0, n - 1)], out_ref.at[pl.ds(0, n - 1)], recv_sem.at[0]).wait()
    local.wait()


def exchange_over_row(pieces):
    n = pieces.shape[0]
    return pl.pallas_call(
        _exchange_kernel,
        out_shape=jax.ShapeDtypeStruct(pieces.shape, pieces.dtype),
        in_specs=[pl.BlockSpec(memory_space=pl.ANY)],
        out_specs=pl.BlockSpec(memory_space=pl.ANY),
        scratch_shapes=[
            pltpu.SemaphoreType.DMA((n - 1,)),
            pltpu.SemaphoreType.DMA((1,)),
            pltpu.SemaphoreType.DMA((1,)),
        ],
        compiler_params=pltpu.CompilerParams(collective_id=0, has_side_effects=True),
    )(pieces)


def per_device(stored, integrals, layout, partner):
    local_rows = stored.shape[0]
    n_z = lax.axis_size("z")
    n_xh = lax.axis_size("xh")
    n_core = lax.axis_size("core")
    n_row = n_z * n_xh * n_core
    n_col = lax.axis_size(COL_AXES)
    total = local_rows * n_row * n_col
    block = total // n_row

    pieces = stored.reshape(local_rows, n_row, stored.shape[1] // n_row).transpose(1, 0, 2)
    regrouped = exchange_over_row(pieces).reshape(n_row * local_rows, pieces.shape[2])
    gathered = lax.all_gather(regrouped, COL_AXES, axis=0, tiled=True)

    s = jnp.arange(total, dtype=jnp.int32)
    s_row = s // (local_rows * n_col)
    s_col = (s // local_rows) % n_col
    s_off = s % local_rows
    pos_of_stored = s_col * (n_row * local_rows) + s_row * local_rows + s_off
    inv = jnp.zeros((total,), jnp.int32).at[layout].set(s)

    i = jnp.arange(total, dtype=jnp.int32)
    g = i // block
    xh = g % n_xh
    core = (g // n_xh) % n_core
    z = g // (n_xh * n_core)
    p_of_i = ((z * n_xh + xh) * n_core + core) * block + (i % block)
    q = partner[p_of_i]

    ladder = jnp.dot(gathered, integrals, preferred_element_type=jnp.float32)
    difference = antisymmetrize(ladder, pos_of_stored[inv[p_of_i]], pos_of_stored[inv[q]])
    part = lax.psum_scatter(difference, ("z", "core"), scatter_dimension=0, tiled=True)
    part = lax.psum_scatter(part, "xh", scatter_dimension=0, tiled=True)
    return part.astype(jnp.bfloat16)


def solution(mesh):
    n_row, n_col = mesh.devices.shape
    fine = Mesh(mesh.devices.reshape(4, n_row // 8, 2, 2, n_col // 2), ROW_AXES + COL_AXES)
    return jax.shard_map(
        per_device,
        mesh=fine,
        in_specs=(P(ROW_AXES + COL_AXES, None), P(ROW_AXES, COL_AXES), P(), P()),
        out_specs=P(ROW_AXES, COL_AXES),
        check_vma=False,
    )
```

```python
import jax
import jax.numpy as jnp
from jax import lax
from jax.experimental import pallas as pl
from jax.experimental.pallas import tpu as pltpu
from jax.sharding import Mesh, PartitionSpec as P

ROW_AXES = ("z", "xh", "core")
COL_AXES = ("xl", "y")


def _antisym_kernel(own_idx, partner_idx, all_ref, out_ref, own_buf, partner_buf, sem):
    rows = out_ref.shape[0]
    step = pl.program_id(0)
    steps = pl.num_programs(0)

    def issue(at, slot):
        base = at * rows

        def body(r, carry):
            pltpu.make_async_copy(all_ref.at[pl.ds(own_idx[base + r], 1)], own_buf.at[slot, pl.ds(r, 1)], sem.at[0, slot]).start()
            pltpu.make_async_copy(all_ref.at[pl.ds(partner_idx[base + r], 1)], partner_buf.at[slot, pl.ds(r, 1)], sem.at[1, slot]).start()
            return carry

        lax.fori_loop(0, rows, body, 0)

    @pl.when(step == 0)
    def _():
        issue(0, 0)

    @pl.when(step + 1 < steps)
    def _():
        issue(step + 1, (step + 1) % 2)

    slot = step % 2
    pltpu.make_async_copy(all_ref.at[pl.ds(0, rows)], own_buf.at[slot], sem.at[0, slot]).wait()
    pltpu.make_async_copy(all_ref.at[pl.ds(0, rows)], partner_buf.at[slot], sem.at[1, slot]).wait()
    out_ref[...] = own_buf[slot] - partner_buf[slot]


def antisymmetrize(ladder, own_rows, partner_rows, rows=64):
    total, width = ladder.shape
    return pl.pallas_call(
        _antisym_kernel,
        grid_spec=pltpu.PrefetchScalarGridSpec(
            num_scalar_prefetch=2,
            grid=(total // rows,),
            in_specs=[pl.BlockSpec(memory_space=pl.ANY)],
            out_specs=pl.BlockSpec((rows, width), lambda b, own, other: (b, 0)),
            scratch_shapes=[
                pltpu.VMEM((2, rows, width), ladder.dtype),
                pltpu.VMEM((2, rows, width), ladder.dtype),
                pltpu.SemaphoreType.DMA((2, 2)),
            ],
        ),
        out_shape=jax.ShapeDtypeStruct(ladder.shape, ladder.dtype),
        compiler_params=pltpu.CompilerParams(dimension_semantics=("arbitrary",)),
        cost_estimate=pl.CostEstimate(flops=total * width, transcendentals=0, bytes_accessed=3 * total * width * 4),
    )(own_rows, partner_rows, ladder)


def _exchange_kernel(src_ref, out_ref, send_sem, recv_sem, local_sem):
    n_z, n_xh, n_core = (lax.axis_size(a) for a in ROW_AXES)
    n = n_z * n_xh * n_core
    z, xh, core, xl, y = (lax.axis_index(a) for a in ROW_AXES + COL_AXES)
    me = (z * n_xh + xh) * n_core + core

    def peer(k):
        t = lax.rem(me + k, n)
        return t, (t // (n_xh * n_core), lax.rem(t // n_core, n_xh), lax.rem(t, n_core), xl, y)

    barrier = pltpu.get_barrier_semaphore()
    for k in range(1, n):
        pl.semaphore_signal(barrier, inc=1, device_id=peer(k)[1], device_id_type=pl.DeviceIdType.MESH)
    pl.semaphore_wait(barrier, n - 1)

    local = pltpu.make_async_copy(src_ref.at[me], out_ref.at[me], local_sem.at[0])
    local.start()
    sends = []
    for k in range(1, n):
        t, where = peer(k)
        copy = pltpu.make_async_remote_copy(
            src_ref=src_ref.at[t],
            dst_ref=out_ref.at[me],
            send_sem=send_sem.at[k - 1],
            recv_sem=recv_sem.at[0],
            device_id=where,
            device_id_type=pl.DeviceIdType.MESH,
        )
        copy.start()
        sends.append(copy)
    for copy in sends:
        copy.wait_send()
    pltpu.make_async_copy(src_ref.at[pl.ds(0, n - 1)], out_ref.at[pl.ds(0, n - 1)], recv_sem.at[0]).wait()
    local.wait()


def exchange_over_row(pieces):
    n = pieces.shape[0]
    return pl.pallas_call(
        _exchange_kernel,
        out_shape=jax.ShapeDtypeStruct(pieces.shape, pieces.dtype),
        in_specs=[pl.BlockSpec(memory_space=pl.ANY)],
        out_specs=pl.BlockSpec(memory_space=pl.ANY),
        scratch_shapes=[
            pltpu.SemaphoreType.DMA((n - 1,)),
            pltpu.SemaphoreType.DMA((1,)),
            pltpu.SemaphoreType.DMA((1,)),
        ],
        compiler_params=pltpu.CompilerParams(collective_id=0, has_side_effects=True),
    )(pieces)


def _pair_sum_kernel(part_ref, out_ref, own_buf, recv_buf, send_sem, recv_sem, local_sem):
    n_xh = lax.axis_size("xh")
    z, xh, core, xl, y = (lax.axis_index(a) for a in ROW_AXES + COL_AXES)
    other = lax.rem(xh + 1, n_xh)
    where = (z, other, core, xl, y)

    barrier = pltpu.get_barrier_semaphore()
    pl.semaphore_signal(barrier, inc=1, device_id=where, device_id_type=pl.DeviceIdType.MESH)
    pl.semaphore_wait(barrier, 1)

    local = pltpu.make_async_copy(part_ref.at[xh], own_buf, local_sem.at[0])
    local.start()
    copy = pltpu.make_async_remote_copy(
        src_ref=part_ref.at[other],
        dst_ref=recv_buf,
        send_sem=send_sem.at[0],
        recv_sem=recv_sem.at[0],
        device_id=where,
        device_id_type=pl.DeviceIdType.MESH,
    )
    copy.start()
    local.wait()
    copy.wait_send()
    copy.wait_recv()
    out_ref[...] = (own_buf[...] + recv_buf[...]).astype(out_ref.dtype)


def sum_over_pair(part):
    _, rows, width = part.shape
    return pl.pallas_call(
        _pair_sum_kernel,
        out_shape=jax.ShapeDtypeStruct((rows, width), jnp.bfloat16),
        in_specs=[pl.BlockSpec(memory_space=pl.ANY)],
        out_specs=pl.BlockSpec(memory_space=pltpu.VMEM),
        scratch_shapes=[
            pltpu.VMEM((rows, width), part.dtype),
            pltpu.VMEM((rows, width), part.dtype),
            pltpu.SemaphoreType.DMA((1,)),
            pltpu.SemaphoreType.DMA((1,)),
            pltpu.SemaphoreType.DMA((1,)),
        ],
        compiler_params=pltpu.CompilerParams(collective_id=1, has_side_effects=True),
    )(part)


def per_device(stored, integrals, layout, partner):
    local_rows = stored.shape[0]
    n_z = lax.axis_size("z")
    n_xh = lax.axis_size("xh")
    n_core = lax.axis_size("core")
    n_row = n_z * n_xh * n_core
    n_col = lax.axis_size(COL_AXES)
    total = local_rows * n_row * n_col
    block = total // n_row

    pieces = stored.reshape(local_rows, n_row, stored.shape[1] // n_row).transpose(1, 0, 2)
    regrouped = exchange_over_row(pieces).reshape(n_row * local_rows, pieces.shape[2])
    gathered = lax.all_gather(regrouped, COL_AXES, axis=0, tiled=True)

    s = jnp.arange(total, dtype=jnp.int32)
    s_row = s // (local_rows * n_col)
    s_col = (s // local_rows) % n_col
    s_off = s % local_rows
    pos_of_stored = s_col * (n_row * local_rows) + s_row * local_rows + s_off
    inv = jnp.zeros((total,), jnp.int32).at[layout].set(s)

    i = jnp.arange(total, dtype=jnp.int32)
    g = i // block
    xh = g % n_xh
    core = (g // n_xh) % n_core
    z = g // (n_xh * n_core)
    p_of_i = ((z * n_xh + xh) * n_core + core) * block + (i % block)
    q = partner[p_of_i]

    ladder = jnp.dot(gathered, integrals, preferred_element_type=jnp.float32)
    difference = antisymmetrize(ladder, pos_of_stored[inv[p_of_i]], pos_of_stored[inv[q]])
    part = lax.psum_scatter(difference, ("z", "core"), scatter_dimension=0, tiled=True)
    return sum_over_pair(part.reshape(n_xh, block, part.shape[1]))


def solution(mesh):
    n_row, n_col = mesh.devices.shape
    fine = Mesh(mesh.devices.reshape(4, n_row // 8, 2, 2, n_col // 2), ROW_AXES + COL_AXES)
    return jax.shard_map(
        per_device,
        mesh=fine,
        in_specs=(P(ROW_AXES + COL_AXES, None), P(ROW_AXES, COL_AXES), P(), P()),
        out_specs=P(ROW_AXES, COL_AXES),
        check_vma=False,
    )
```

```python
import jax
import jax.numpy as jnp
from jax import lax
from jax.experimental import pallas as pl
from jax.experimental.pallas import tpu as pltpu
from jax.sharding import Mesh, PartitionSpec as P

ROW_AXES = ("z", "xh", "core")
COL_AXES = ("xl", "y")


def _antisym_kernel(own_idx, partner_idx, all_ref, out_ref, own_buf, partner_buf, sem):
    rows = out_ref.shape[0]
    step = pl.program_id(0)
    steps = pl.num_programs(0)

    def issue(at, slot):
        base = at * rows

        def body(r, carry):
            pltpu.make_async_copy(all_ref.at[pl.ds(own_idx[base + r], 1)], own_buf.at[slot, pl.ds(r, 1)], sem.at[0, slot]).start()
            pltpu.make_async_copy(all_ref.at[pl.ds(partner_idx[base + r], 1)], partner_buf.at[slot, pl.ds(r, 1)], sem.at[1, slot]).start()
            return carry

        lax.fori_loop(0, rows, body, 0)

    @pl.when(step == 0)
    def _():
        issue(0, 0)

    @pl.when(step + 1 < steps)
    def _():
        issue(step + 1, (step + 1) % 2)

    slot = step % 2
    pltpu.make_async_copy(all_ref.at[pl.ds(0, rows)], own_buf.at[slot], sem.at[0, slot]).wait()
    pltpu.make_async_copy(all_ref.at[pl.ds(0, rows)], partner_buf.at[slot], sem.at[1, slot]).wait()
    out_ref[...] = own_buf[slot] - partner_buf[slot]


def antisymmetrize(ladder, own_rows, partner_rows, rows=64):
    total, width = ladder.shape
    return pl.pallas_call(
        _antisym_kernel,
        grid_spec=pltpu.PrefetchScalarGridSpec(
            num_scalar_prefetch=2,
            grid=(total // rows,),
            in_specs=[pl.BlockSpec(memory_space=pl.ANY)],
            out_specs=pl.BlockSpec((rows, width), lambda b, own, other: (b, 0)),
            scratch_shapes=[
                pltpu.VMEM((2, rows, width), ladder.dtype),
                pltpu.VMEM((2, rows, width), ladder.dtype),
                pltpu.SemaphoreType.DMA((2, 2)),
            ],
        ),
        out_shape=jax.ShapeDtypeStruct(ladder.shape, ladder.dtype),
        compiler_params=pltpu.CompilerParams(dimension_semantics=("arbitrary",)),
        cost_estimate=pl.CostEstimate(flops=total * width, transcendentals=0, bytes_accessed=3 * total * width * 4),
    )(own_rows, partner_rows, ladder)


def _exchange_kernel(src_ref, out_ref, send_sem, recv_sem, local_sem):
    n_z, n_xh, n_core = (lax.axis_size(a) for a in ROW_AXES)
    n = n_z * n_xh * n_core
    z, xh, core, xl, y = (lax.axis_index(a) for a in ROW_AXES + COL_AXES)
    me = (z * n_xh + xh) * n_core + core

    def peer(k):
        t = lax.rem(me + k, n)
        return t, (t // (n_xh * n_core), lax.rem(t // n_core, n_xh), lax.rem(t, n_core), xl, y)

    barrier = pltpu.get_barrier_semaphore()
    for k in range(1, n):
        pl.semaphore_signal(barrier, inc=1, device_id=peer(k)[1], device_id_type=pl.DeviceIdType.MESH)
    pl.semaphore_wait(barrier, n - 1)

    local = pltpu.make_async_copy(src_ref.at[me], out_ref.at[me], local_sem.at[0])
    local.start()
    sends = []
    for k in range(1, n):
        t, where = peer(k)
        copy = pltpu.make_async_remote_copy(
            src_ref=src_ref.at[t],
            dst_ref=out_ref.at[me],
            send_sem=send_sem.at[k - 1],
            recv_sem=recv_sem.at[0],
            device_id=where,
            device_id_type=pl.DeviceIdType.MESH,
        )
        copy.start()
        sends.append(copy)
    for copy in sends:
        copy.wait_send()
    pltpu.make_async_copy(src_ref.at[pl.ds(0, n - 1)], out_ref.at[pl.ds(0, n - 1)], recv_sem.at[0]).wait()
    local.wait()


def exchange_over_row(pieces):
    n = pieces.shape[0]
    return pl.pallas_call(
        _exchange_kernel,
        out_shape=jax.ShapeDtypeStruct(pieces.shape, pieces.dtype),
        in_specs=[pl.BlockSpec(memory_space=pl.ANY)],
        out_specs=pl.BlockSpec(memory_space=pl.ANY),
        scratch_shapes=[
            pltpu.SemaphoreType.DMA((n - 1,)),
            pltpu.SemaphoreType.DMA((1,)),
            pltpu.SemaphoreType.DMA((1,)),
        ],
        compiler_params=pltpu.CompilerParams(collective_id=0, has_side_effects=True),
    )(pieces)


def _pair_sum_kernel(part_ref, out_ref, own_buf, recv_buf, send_sem, recv_sem, local_sem):
    n_xh = lax.axis_size("xh")
    z, xh, core, xl, y = (lax.axis_index(a) for a in ROW_AXES + COL_AXES)
    other = lax.rem(xh + 1, n_xh)
    where = (z, other, core, xl, y)
    pieces = send_sem.shape[0]
    rows = own_buf.shape[0] // pieces

    barrier = pltpu.get_barrier_semaphore()
    pl.semaphore_signal(barrier, inc=1, device_id=where, device_id_type=pl.DeviceIdType.MESH)
    pl.semaphore_wait(barrier, 1)

    local = pltpu.make_async_copy(part_ref.at[xh], own_buf, local_sem.at[0])
    local.start()
    sends = []
    for k in range(pieces):
        copy = pltpu.make_async_remote_copy(
            src_ref=part_ref.at[other, pl.ds(k * rows, rows)],
            dst_ref=recv_buf.at[pl.ds(k * rows, rows)],
            send_sem=send_sem.at[k],
            recv_sem=recv_sem.at[0],
            device_id=where,
            device_id_type=pl.DeviceIdType.MESH,
        )
        copy.start()
        sends.append(copy)
    local.wait()
    for copy in sends:
        copy.wait_send()
    pltpu.make_async_copy(part_ref.at[xh], recv_buf, recv_sem.at[0]).wait()
    out_ref[...] = (own_buf[...] + recv_buf[...]).astype(out_ref.dtype)


def sum_over_pair(part, pieces=4):
    _, rows, width = part.shape
    return pl.pallas_call(
        _pair_sum_kernel,
        out_shape=jax.ShapeDtypeStruct((rows, width), jnp.bfloat16),
        in_specs=[pl.BlockSpec(memory_space=pl.ANY)],
        out_specs=pl.BlockSpec(memory_space=pltpu.VMEM),
        scratch_shapes=[
            pltpu.VMEM((rows, width), part.dtype),
            pltpu.VMEM((rows, width), part.dtype),
            pltpu.SemaphoreType.DMA((pieces,)),
            pltpu.SemaphoreType.DMA((1,)),
            pltpu.SemaphoreType.DMA((1,)),
        ],
        compiler_params=pltpu.CompilerParams(collective_id=1, has_side_effects=True),
    )(part)


def per_device(stored, integrals, layout, partner):
    local_rows = stored.shape[0]
    n_z = lax.axis_size("z")
    n_xh = lax.axis_size("xh")
    n_core = lax.axis_size("core")
    n_row = n_z * n_xh * n_core
    n_col = lax.axis_size(COL_AXES)
    total = local_rows * n_row * n_col
    block = total // n_row

    pieces = stored.reshape(local_rows, n_row, stored.shape[1] // n_row).transpose(1, 0, 2)
    regrouped = exchange_over_row(pieces).reshape(n_row * local_rows, pieces.shape[2])
    gathered = lax.all_gather(regrouped, COL_AXES, axis=0, tiled=True)

    s = jnp.arange(total, dtype=jnp.int32)
    s_row = s // (local_rows * n_col)
    s_col = (s // local_rows) % n_col
    s_off = s % local_rows
    pos_of_stored = s_col * (n_row * local_rows) + s_row * local_rows + s_off
    inv = jnp.zeros((total,), jnp.int32).at[layout].set(s)

    i = jnp.arange(total, dtype=jnp.int32)
    g = i // block
    xh = g % n_xh
    core = (g // n_xh) % n_core
    z = g // (n_xh * n_core)
    p_of_i = ((z * n_xh + xh) * n_core + core) * block + (i % block)
    q = partner[p_of_i]

    ladder = jnp.dot(gathered, integrals, preferred_element_type=jnp.float32)
    difference = antisymmetrize(ladder, pos_of_stored[inv[p_of_i]], pos_of_stored[inv[q]])
    part = lax.psum_scatter(difference, ("z", "core"), scatter_dimension=0, tiled=True)
    return sum_over_pair(part.reshape(n_xh, block, part.shape[1]))


def solution(mesh):
    n_row, n_col = mesh.devices.shape
    fine = Mesh(mesh.devices.reshape(4, n_row // 8, 2, 2, n_col // 2), ROW_AXES + COL_AXES)
    return jax.shard_map(
        per_device,
        mesh=fine,
        in_specs=(P(ROW_AXES + COL_AXES, None), P(ROW_AXES, COL_AXES), P(), P()),
        out_specs=P(ROW_AXES, COL_AXES),
        check_vma=False,
    )
```

```python
import jax
import jax.numpy as jnp
from jax import lax
from jax.experimental import pallas as pl
from jax.experimental.pallas import tpu as pltpu
from jax.sharding import Mesh, PartitionSpec as P

ROW_AXES = ("z", "xh", "core")
COL_AXES = ("xl", "y")


def _antisym_kernel(own_idx, partner_idx, all_ref, out_ref, own_buf, partner_buf, sem):
    rows = out_ref.shape[0]
    step = pl.program_id(0)
    steps = pl.num_programs(0)

    def issue(at, slot):
        base = at * rows

        def body(r, carry):
            pltpu.make_async_copy(all_ref.at[pl.ds(own_idx[base + r], 1)], own_buf.at[slot, pl.ds(r, 1)], sem.at[0, slot]).start()
            pltpu.make_async_copy(all_ref.at[pl.ds(partner_idx[base + r], 1)], partner_buf.at[slot, pl.ds(r, 1)], sem.at[1, slot]).start()
            return carry

        lax.fori_loop(0, rows, body, 0)

    @pl.when(step == 0)
    def _():
        issue(0, 0)

    @pl.when(step + 1 < steps)
    def _():
        issue(step + 1, (step + 1) % 2)

    slot = step % 2
    pltpu.make_async_copy(all_ref.at[pl.ds(0, rows)], own_buf.at[slot], sem.at[0, slot]).wait()
    pltpu.make_async_copy(all_ref.at[pl.ds(0, rows)], partner_buf.at[slot], sem.at[1, slot]).wait()
    out_ref[...] = own_buf[slot] - partner_buf[slot]


def antisymmetrize(ladder, own_rows, partner_rows, rows=128):
    total, width = ladder.shape
    return pl.pallas_call(
        _antisym_kernel,
        grid_spec=pltpu.PrefetchScalarGridSpec(
            num_scalar_prefetch=2,
            grid=(total // rows,),
            in_specs=[pl.BlockSpec(memory_space=pl.ANY)],
            out_specs=pl.BlockSpec((rows, width), lambda b, own, other: (b, 0)),
            scratch_shapes=[
                pltpu.VMEM((2, rows, width), ladder.dtype),
                pltpu.VMEM((2, rows, width), ladder.dtype),
                pltpu.SemaphoreType.DMA((2, 2)),
            ],
        ),
        out_shape=jax.ShapeDtypeStruct(ladder.shape, ladder.dtype),
        compiler_params=pltpu.CompilerParams(dimension_semantics=("arbitrary",)),
        cost_estimate=pl.CostEstimate(flops=total * width, transcendentals=0, bytes_accessed=3 * total * width * 4),
    )(own_rows, partner_rows, ladder)


def _exchange_kernel(src_ref, out_ref, send_sem, recv_sem, local_sem):
    n_z, n_xh, n_core = (lax.axis_size(a) for a in ROW_AXES)
    n = n_z * n_xh * n_core
    z, xh, core, xl, y = (lax.axis_index(a) for a in ROW_AXES + COL_AXES)
    me = (z * n_xh + xh) * n_core + core

    def peer(k):
        t = lax.rem(me + k, n)
        return t, (t // (n_xh * n_core), lax.rem(t // n_core, n_xh), lax.rem(t, n_core), xl, y)

    barrier = pltpu.get_barrier_semaphore()
    for k in range(1, n):
        pl.semaphore_signal(barrier, inc=1, device_id=peer(k)[1], device_id_type=pl.DeviceIdType.MESH)
    pl.semaphore_wait(barrier, n - 1)

    local = pltpu.make_async_copy(src_ref.at[me], out_ref.at[me], local_sem.at[0])
    local.start()
    sends = []
    for k in range(1, n):
        t, where = peer(k)
        copy = pltpu.make_async_remote_copy(
            src_ref=src_ref.at[t],
            dst_ref=out_ref.at[me],
            send_sem=send_sem.at[k - 1],
            recv_sem=recv_sem.at[0],
            device_id=where,
            device_id_type=pl.DeviceIdType.MESH,
        )
        copy.start()
        sends.append(copy)
    for copy in sends:
        copy.wait_send()
    pltpu.make_async_copy(src_ref.at[pl.ds(0, n - 1)], out_ref.at[pl.ds(0, n - 1)], recv_sem.at[0]).wait()
    local.wait()


def exchange_over_row(pieces):
    n = pieces.shape[0]
    return pl.pallas_call(
        _exchange_kernel,
        out_shape=jax.ShapeDtypeStruct(pieces.shape, pieces.dtype),
        in_specs=[pl.BlockSpec(memory_space=pl.ANY)],
        out_specs=pl.BlockSpec(memory_space=pl.ANY),
        scratch_shapes=[
            pltpu.SemaphoreType.DMA((n - 1,)),
            pltpu.SemaphoreType.DMA((1,)),
            pltpu.SemaphoreType.DMA((1,)),
        ],
        compiler_params=pltpu.CompilerParams(collective_id=0, has_side_effects=True),
    )(pieces)


def _pair_sum_kernel(part_ref, out_ref, own_buf, recv_buf, send_sem, recv_sem, local_sem):
    n_xh = lax.axis_size("xh")
    z, xh, core, xl, y = (lax.axis_index(a) for a in ROW_AXES + COL_AXES)
    other = lax.rem(xh + 1, n_xh)
    where = (z, other, core, xl, y)
    pieces = send_sem.shape[0]
    rows = own_buf.shape[0] // pieces

    barrier = pltpu.get_barrier_semaphore()
    pl.semaphore_signal(barrier, inc=1, device_id=where, device_id_type=pl.DeviceIdType.MESH)
    pl.semaphore_wait(barrier, 1)

    local = pltpu.make_async_copy(part_ref.at[xh], own_buf, local_sem.at[0])
    local.start()
    sends = []
    for k in range(pieces):
        copy = pltpu.make_async_remote_copy(
            src_ref=part_ref.at[other, pl.ds(k * rows, rows)],
            dst_ref=recv_buf.at[pl.ds(k * rows, rows)],
            send_sem=send_sem.at[k],
            recv_sem=recv_sem.at[0],
            device_id=where,
            device_id_type=pl.DeviceIdType.MESH,
        )
        copy.start()
        sends.append(copy)
    local.wait()
    for copy in sends:
        copy.wait_send()
    pltpu.make_async_copy(part_ref.at[xh], recv_buf, recv_sem.at[0]).wait()
    out_ref[...] = (own_buf[...] + recv_buf[...]).astype(out_ref.dtype)


def sum_over_pair(part, pieces=4):
    _, rows, width = part.shape
    return pl.pallas_call(
        _pair_sum_kernel,
        out_shape=jax.ShapeDtypeStruct((rows, width), jnp.bfloat16),
        in_specs=[pl.BlockSpec(memory_space=pl.ANY)],
        out_specs=pl.BlockSpec(memory_space=pltpu.VMEM),
        scratch_shapes=[
            pltpu.VMEM((rows, width), part.dtype),
            pltpu.VMEM((rows, width), part.dtype),
            pltpu.SemaphoreType.DMA((pieces,)),
            pltpu.SemaphoreType.DMA((1,)),
            pltpu.SemaphoreType.DMA((1,)),
        ],
        compiler_params=pltpu.CompilerParams(collective_id=1, has_side_effects=True),
    )(part)


def per_device(stored, integrals, layout, partner):
    local_rows = stored.shape[0]
    n_z = lax.axis_size("z")
    n_xh = lax.axis_size("xh")
    n_core = lax.axis_size("core")
    n_row = n_z * n_xh * n_core
    n_col = lax.axis_size(COL_AXES)
    total = local_rows * n_row * n_col
    block = total // n_row

    pieces = stored.reshape(local_rows, n_row, stored.shape[1] // n_row).transpose(1, 0, 2)
    regrouped = exchange_over_row(pieces).reshape(n_row * local_rows, pieces.shape[2])
    gathered = lax.all_gather(regrouped, COL_AXES, axis=0, tiled=True)

    s = jnp.arange(total, dtype=jnp.int32)
    s_row = s // (local_rows * n_col)
    s_col = (s // local_rows) % n_col
    s_off = s % local_rows
    pos_of_stored = s_col * (n_row * local_rows) + s_row * local_rows + s_off
    inv = jnp.zeros((total,), jnp.int32).at[layout].set(s)

    i = jnp.arange(total, dtype=jnp.int32)
    g = i // block
    xh = g % n_xh
    core = (g // n_xh) % n_core
    z = g // (n_xh * n_core)
    p_of_i = ((z * n_xh + xh) * n_core + core) * block + (i % block)
    q = partner[p_of_i]

    ladder = jnp.dot(gathered, integrals, preferred_element_type=jnp.float32)
    difference = antisymmetrize(ladder, pos_of_stored[inv[p_of_i]], pos_of_stored[inv[q]])
    part = lax.psum_scatter(difference, ("z", "core"), scatter_dimension=0, tiled=True)
    return sum_over_pair(part.reshape(n_xh, block, part.shape[1]))


def solution(mesh):
    n_row, n_col = mesh.devices.shape
    fine = Mesh(mesh.devices.reshape(4, n_row // 8, 2, 2, n_col // 2), ROW_AXES + COL_AXES)
    return jax.shard_map(
        per_device,
        mesh=fine,
        in_specs=(P(ROW_AXES + COL_AXES, None), P(ROW_AXES, COL_AXES), P(), P()),
        out_specs=P(ROW_AXES, COL_AXES),
        check_vma=False,
    )
```

```python
import jax
import jax.numpy as jnp
from jax import lax
from jax.experimental import pallas as pl
from jax.experimental.pallas import tpu as pltpu
from jax.sharding import Mesh, PartitionSpec as P

ROW_AXES = ("z", "xh", "core")
COL_AXES = ("xl", "y")


def _antisym_kernel(own_idx, partner_idx, all_ref, out_ref, own_buf, partner_buf, sem):
    rows = out_ref.shape[0]
    step = pl.program_id(0)
    steps = pl.num_programs(0)

    def issue(at, slot):
        base = at * rows

        def body(r, carry):
            pltpu.make_async_copy(all_ref.at[pl.ds(own_idx[base + r], 1)], own_buf.at[slot, pl.ds(r, 1)], sem.at[0, slot]).start()
            pltpu.make_async_copy(all_ref.at[pl.ds(partner_idx[base + r], 1)], partner_buf.at[slot, pl.ds(r, 1)], sem.at[1, slot]).start()
            return carry

        lax.fori_loop(0, rows, body, 0)

    @pl.when(step == 0)
    def _():
        issue(0, 0)

    @pl.when(step + 1 < steps)
    def _():
        issue(step + 1, (step + 1) % 2)

    slot = step % 2
    pltpu.make_async_copy(all_ref.at[pl.ds(0, rows)], own_buf.at[slot], sem.at[0, slot]).wait()
    pltpu.make_async_copy(all_ref.at[pl.ds(0, rows)], partner_buf.at[slot], sem.at[1, slot]).wait()
    out_ref[...] = own_buf[slot] - partner_buf[slot]


def antisymmetrize(ladder, own_rows, partner_rows, rows=128):
    total, width = ladder.shape
    return pl.pallas_call(
        _antisym_kernel,
        grid_spec=pltpu.PrefetchScalarGridSpec(
            num_scalar_prefetch=2,
            grid=(total // rows,),
            in_specs=[pl.BlockSpec(memory_space=pl.ANY)],
            out_specs=pl.BlockSpec((rows, width), lambda b, own, other: (b, 0)),
            scratch_shapes=[
                pltpu.VMEM((2, rows, width), ladder.dtype),
                pltpu.VMEM((2, rows, width), ladder.dtype),
                pltpu.SemaphoreType.DMA((2, 2)),
            ],
        ),
        out_shape=jax.ShapeDtypeStruct(ladder.shape, ladder.dtype),
        compiler_params=pltpu.CompilerParams(dimension_semantics=("arbitrary",)),
        cost_estimate=pl.CostEstimate(flops=total * width, transcendentals=0, bytes_accessed=3 * total * width * 4),
    )(own_rows, partner_rows, ladder)


def _spread_kernel(src_ref, out_ref, send_sem, recv_sem, local_sem):
    n_z, n_xh, n_core, n_xl, n_y = (lax.axis_size(a) for a in ROW_AXES + COL_AXES)
    n_col = n_xl * n_y
    n = n_z * n_xh * n_core * n_col
    z, xh, core, xl, y = (lax.axis_index(a) for a in ROW_AXES + COL_AXES)
    me = ((z * n_xh + xh) * n_core + core) * n_col + xl * n_y + y

    def peer(k):
        t = lax.rem(me + k, n)
        r, c = t // n_col, lax.rem(t, n_col)
        return r, (r // (n_xh * n_core), lax.rem(r // n_core, n_xh), lax.rem(r, n_core), c // n_y, lax.rem(c, n_y))

    barrier = pltpu.get_barrier_semaphore()

    def signal(k, carry):
        pl.semaphore_signal(barrier, inc=1, device_id=peer(k)[1], device_id_type=pl.DeviceIdType.MESH)
        return carry

    lax.fori_loop(1, n, signal, 0)
    pl.semaphore_wait(barrier, n - 1)

    local = pltpu.make_async_copy(src_ref.at[me // n_col], out_ref.at[me], local_sem.at[0])
    local.start()

    def send(k):
        r, where = peer(k)
        return pltpu.make_async_remote_copy(
            src_ref=src_ref.at[r],
            dst_ref=out_ref.at[me],
            send_sem=send_sem.at[k - 1],
            recv_sem=recv_sem.at[0],
            device_id=where,
            device_id_type=pl.DeviceIdType.MESH,
        )

    def start(k, carry):
        send(k).start()
        return carry

    def finish(k, carry):
        send(k).wait_send()
        return carry

    lax.fori_loop(1, n, start, 0)
    lax.fori_loop(1, n, finish, 0)
    pltpu.make_async_copy(out_ref.at[pl.ds(0, n - 1)], out_ref.at[pl.ds(0, n - 1)], recv_sem.at[0]).wait()
    local.wait()


def spread(pieces, devices):
    _, rows, width = pieces.shape
    return pl.pallas_call(
        _spread_kernel,
        out_shape=jax.ShapeDtypeStruct((devices, rows, width), pieces.dtype),
        in_specs=[pl.BlockSpec(memory_space=pl.ANY)],
        out_specs=pl.BlockSpec(memory_space=pl.ANY),
        scratch_shapes=[
            pltpu.SemaphoreType.DMA((devices - 1,)),
            pltpu.SemaphoreType.DMA((1,)),
            pltpu.SemaphoreType.DMA((1,)),
        ],
        compiler_params=pltpu.CompilerParams(collective_id=0, has_side_effects=True),
    )(pieces)


def _lookup(table, index):
    hits = index[:, None] == jnp.arange(table.shape[0], dtype=jnp.int32)[None, :]
    return jnp.sum(jnp.where(hits, table[None, :], 0), axis=1)


def _inverse(perm):
    hits = perm[None, :] == jnp.arange(perm.shape[0], dtype=jnp.int32)[:, None]
    return jnp.sum(jnp.where(hits, jnp.arange(perm.shape[0], dtype=jnp.int32)[None, :], 0), axis=1)


def _pair_sum_kernel(part_ref, out_ref, own_buf, recv_buf, send_sem, recv_sem, local_sem):
    n_xh = lax.axis_size("xh")
    z, xh, core, xl, y = (lax.axis_index(a) for a in ROW_AXES + COL_AXES)
    other = lax.rem(xh + 1, n_xh)
    where = (z, other, core, xl, y)
    pieces = send_sem.shape[0]
    rows = own_buf.shape[0] // pieces

    barrier = pltpu.get_barrier_semaphore()
    pl.semaphore_signal(barrier, inc=1, device_id=where, device_id_type=pl.DeviceIdType.MESH)
    pl.semaphore_wait(barrier, 1)

    local = pltpu.make_async_copy(part_ref.at[xh], own_buf, local_sem.at[0])
    local.start()
    sends = []
    for k in range(pieces):
        copy = pltpu.make_async_remote_copy(
            src_ref=part_ref.at[other, pl.ds(k * rows, rows)],
            dst_ref=recv_buf.at[pl.ds(k * rows, rows)],
            send_sem=send_sem.at[k],
            recv_sem=recv_sem.at[0],
            device_id=where,
            device_id_type=pl.DeviceIdType.MESH,
        )
        copy.start()
        sends.append(copy)
    local.wait()
    for copy in sends:
        copy.wait_send()
    pltpu.make_async_copy(part_ref.at[xh], recv_buf, recv_sem.at[0]).wait()
    out_ref[...] = (own_buf[...] + recv_buf[...]).astype(out_ref.dtype)


def sum_over_pair(part, pieces=4):
    _, rows, width = part.shape
    return pl.pallas_call(
        _pair_sum_kernel,
        out_shape=jax.ShapeDtypeStruct((rows, width), jnp.bfloat16),
        in_specs=[pl.BlockSpec(memory_space=pl.ANY)],
        out_specs=pl.BlockSpec(memory_space=pltpu.VMEM),
        scratch_shapes=[
            pltpu.VMEM((rows, width), part.dtype),
            pltpu.VMEM((rows, width), part.dtype),
            pltpu.SemaphoreType.DMA((pieces,)),
            pltpu.SemaphoreType.DMA((1,)),
            pltpu.SemaphoreType.DMA((1,)),
        ],
        compiler_params=pltpu.CompilerParams(collective_id=1, has_side_effects=True),
    )(part)


def per_device(stored, integrals, layout, partner):
    local_rows = stored.shape[0]
    n_z = lax.axis_size("z")
    n_xh = lax.axis_size("xh")
    n_core = lax.axis_size("core")
    n_row = n_z * n_xh * n_core
    n_col = lax.axis_size(COL_AXES)
    total = local_rows * n_row * n_col
    block = total // n_row

    pieces = stored.reshape(local_rows, n_row, stored.shape[1] // n_row).transpose(1, 0, 2)
    gathered = spread(pieces, n_row * n_col).reshape(total, pieces.shape[2])
    inv = _inverse(layout)

    i = jnp.arange(total, dtype=jnp.int32)
    g = i // block
    xh = g % n_xh
    core = (g // n_xh) % n_core
    z = g // (n_xh * n_core)
    p_of_i = ((z * n_xh + xh) * n_core + core) * block + (i % block)
    q = _lookup(partner, p_of_i)

    ladder = jnp.dot(gathered, integrals, preferred_element_type=jnp.float32)
    difference = antisymmetrize(ladder, _lookup(inv, p_of_i), _lookup(inv, q))
    part = lax.psum_scatter(difference, ("z", "core"), scatter_dimension=0, tiled=True)
    return sum_over_pair(part.reshape(n_xh, block, part.shape[1]))


def solution(mesh):
    n_row, n_col = mesh.devices.shape
    fine = Mesh(mesh.devices.reshape(4, n_row // 8, 2, 2, n_col // 2), ROW_AXES + COL_AXES)
    return jax.shard_map(
        per_device,
        mesh=fine,
        in_specs=(P(ROW_AXES + COL_AXES, None), P(ROW_AXES, COL_AXES), P(), P()),
        out_specs=P(ROW_AXES, COL_AXES),
        check_vma=False,
    )
```

```python
import jax
import jax.numpy as jnp
from jax import lax
from jax.experimental import pallas as pl
from jax.experimental.pallas import tpu as pltpu
from jax.sharding import Mesh, PartitionSpec as P

ROW_AXES = ("z", "xh", "core")
COL_AXES = ("xl", "y")


def _antisym_kernel(own_idx, partner_idx, all_ref, out_ref, own_buf, partner_buf, sem):
    rows = out_ref.shape[0]
    step = pl.program_id(0)
    steps = pl.num_programs(0)

    def issue(at, slot):
        base = at * rows

        def body(r, carry):
            pltpu.make_async_copy(all_ref.at[pl.ds(own_idx[base + r], 1)], own_buf.at[slot, pl.ds(r, 1)], sem.at[0, slot]).start()
            pltpu.make_async_copy(all_ref.at[pl.ds(partner_idx[base + r], 1)], partner_buf.at[slot, pl.ds(r, 1)], sem.at[1, slot]).start()
            return carry

        lax.fori_loop(0, rows, body, 0)

    @pl.when(step == 0)
    def _():
        issue(0, 0)

    @pl.when(step + 1 < steps)
    def _():
        issue(step + 1, (step + 1) % 2)

    slot = step % 2
    pltpu.make_async_copy(all_ref.at[pl.ds(0, rows)], own_buf.at[slot], sem.at[0, slot]).wait()
    pltpu.make_async_copy(all_ref.at[pl.ds(0, rows)], partner_buf.at[slot], sem.at[1, slot]).wait()
    out_ref[...] = own_buf[slot] - partner_buf[slot]


def antisymmetrize(ladder, own_rows, partner_rows, rows=128):
    total, width = ladder.shape
    return pl.pallas_call(
        _antisym_kernel,
        grid_spec=pltpu.PrefetchScalarGridSpec(
            num_scalar_prefetch=2,
            grid=(total // rows,),
            in_specs=[pl.BlockSpec(memory_space=pl.ANY)],
            out_specs=pl.BlockSpec((rows, width), lambda b, own, other: (b, 0)),
            scratch_shapes=[
                pltpu.VMEM((2, rows, width), ladder.dtype),
                pltpu.VMEM((2, rows, width), ladder.dtype),
                pltpu.SemaphoreType.DMA((2, 2)),
            ],
        ),
        out_shape=jax.ShapeDtypeStruct(ladder.shape, ladder.dtype),
        compiler_params=pltpu.CompilerParams(dimension_semantics=("arbitrary",)),
        cost_estimate=pl.CostEstimate(flops=total * width, transcendentals=0, bytes_accessed=3 * total * width * 4),
    )(own_rows, partner_rows, ladder)


def _exchange_kernel(src_ref, out_ref, send_sem, recv_sem, local_sem):
    n_z, n_xh, n_core = (lax.axis_size(a) for a in ROW_AXES)
    n = n_z * n_xh * n_core
    z, xh, core, xl, y = (lax.axis_index(a) for a in ROW_AXES + COL_AXES)
    me = (z * n_xh + xh) * n_core + core

    def peer(k):
        t = lax.rem(me + k, n)
        return t, (t // (n_xh * n_core), lax.rem(t // n_core, n_xh), lax.rem(t, n_core), xl, y)

    barrier = pltpu.get_barrier_semaphore()
    for k in range(1, n):
        pl.semaphore_signal(barrier, inc=1, device_id=peer(k)[1], device_id_type=pl.DeviceIdType.MESH)
    pl.semaphore_wait(barrier, n - 1)

    local = pltpu.make_async_copy(src_ref.at[me], out_ref.at[me], local_sem.at[0])
    local.start()
    sends = []
    for k in range(1, n):
        t, where = peer(k)
        copy = pltpu.make_async_remote_copy(
            src_ref=src_ref.at[t],
            dst_ref=out_ref.at[me],
            send_sem=send_sem.at[k - 1],
            recv_sem=recv_sem.at[0],
            device_id=where,
            device_id_type=pl.DeviceIdType.MESH,
        )
        copy.start()
        sends.append(copy)
    for copy in sends:
        copy.wait_send()
    pltpu.make_async_copy(src_ref.at[pl.ds(0, n - 1)], out_ref.at[pl.ds(0, n - 1)], recv_sem.at[0]).wait()
    local.wait()


def exchange_over_row(pieces):
    n = pieces.shape[0]
    return pl.pallas_call(
        _exchange_kernel,
        out_shape=jax.ShapeDtypeStruct(pieces.shape, pieces.dtype),
        in_specs=[pl.BlockSpec(memory_space=pl.ANY)],
        out_specs=pl.BlockSpec(memory_space=pl.ANY),
        scratch_shapes=[
            pltpu.SemaphoreType.DMA((n - 1,)),
            pltpu.SemaphoreType.DMA((1,)),
            pltpu.SemaphoreType.DMA((1,)),
        ],
        compiler_params=pltpu.CompilerParams(collective_id=0, has_side_effects=True),
    )(pieces)


def _col_gather_kernel(src_ref, out_ref, send_sem, recv_sem, local_sem):
    n_xl, n_y = (lax.axis_size(a) for a in COL_AXES)
    n = n_xl * n_y
    z, xh, core, xl, y = (lax.axis_index(a) for a in ROW_AXES + COL_AXES)
    me = xl * n_y + y

    def peer(k):
        t = lax.rem(me + k, n)
        return (z, xh, core, t // n_y, lax.rem(t, n_y))

    barrier = pltpu.get_barrier_semaphore()
    for k in range(1, n):
        pl.semaphore_signal(barrier, inc=1, device_id=peer(k), device_id_type=pl.DeviceIdType.MESH)
    pl.semaphore_wait(barrier, n - 1)

    local = pltpu.make_async_copy(src_ref, out_ref.at[me], local_sem.at[0])
    local.start()
    sends = []
    for k in range(1, n):
        copy = pltpu.make_async_remote_copy(
            src_ref=src_ref,
            dst_ref=out_ref.at[me],
            send_sem=send_sem.at[k - 1],
            recv_sem=recv_sem.at[0],
            device_id=peer(k),
            device_id_type=pl.DeviceIdType.MESH,
        )
        copy.start()
        sends.append(copy)
    for copy in sends:
        copy.wait_send()
    pltpu.make_async_copy(out_ref.at[pl.ds(0, n - 1)], out_ref.at[pl.ds(0, n - 1)], recv_sem.at[0]).wait()
    local.wait()


def gather_over_col(block, n):
    return pl.pallas_call(
        _col_gather_kernel,
        out_shape=jax.ShapeDtypeStruct((n,) + block.shape, block.dtype),
        in_specs=[pl.BlockSpec(memory_space=pl.ANY)],
        out_specs=pl.BlockSpec(memory_space=pl.ANY),
        scratch_shapes=[
            pltpu.SemaphoreType.DMA((n - 1,)),
            pltpu.SemaphoreType.DMA((1,)),
            pltpu.SemaphoreType.DMA((1,)),
        ],
        compiler_params=pltpu.CompilerParams(collective_id=2, has_side_effects=True),
    )(block)


def _lookup(table, index):
    hits = index[:, None] == jnp.arange(table.shape[0], dtype=jnp.int32)[None, :]
    return jnp.sum(jnp.where(hits, table[None, :], 0), axis=1)


def _inverse(perm):
    hits = perm[None, :] == jnp.arange(perm.shape[0], dtype=jnp.int32)[:, None]
    return jnp.sum(jnp.where(hits, jnp.arange(perm.shape[0], dtype=jnp.int32)[None, :], 0), axis=1)


def _pair_sum_kernel(part_ref, out_ref, own_buf, recv_buf, send_sem, recv_sem, local_sem):
    n_xh = lax.axis_size("xh")
    z, xh, core, xl, y = (lax.axis_index(a) for a in ROW_AXES + COL_AXES)
    other = lax.rem(xh + 1, n_xh)
    where = (z, other, core, xl, y)
    pieces = send_sem.shape[0]
    rows = own_buf.shape[0] // pieces

    barrier = pltpu.get_barrier_semaphore()
    pl.semaphore_signal(barrier, inc=1, device_id=where, device_id_type=pl.DeviceIdType.MESH)
    pl.semaphore_wait(barrier, 1)

    local = pltpu.make_async_copy(part_ref.at[xh], own_buf, local_sem.at[0])
    local.start()
    sends = []
    for k in range(pieces):
        copy = pltpu.make_async_remote_copy(
            src_ref=part_ref.at[other, pl.ds(k * rows, rows)],
            dst_ref=recv_buf.at[pl.ds(k * rows, rows)],
            send_sem=send_sem.at[k],
            recv_sem=recv_sem.at[0],
            device_id=where,
            device_id_type=pl.DeviceIdType.MESH,
        )
        copy.start()
        sends.append(copy)
    local.wait()
    for copy in sends:
        copy.wait_send()
    pltpu.make_async_copy(part_ref.at[xh], recv_buf, recv_sem.at[0]).wait()
    out_ref[...] = (own_buf[...] + recv_buf[...]).astype(out_ref.dtype)


def sum_over_pair(part, pieces=4):
    _, rows, width = part.shape
    return pl.pallas_call(
        _pair_sum_kernel,
        out_shape=jax.ShapeDtypeStruct((rows, width), jnp.bfloat16),
        in_specs=[pl.BlockSpec(memory_space=pl.ANY)],
        out_specs=pl.BlockSpec(memory_space=pltpu.VMEM),
        scratch_shapes=[
            pltpu.VMEM((rows, width), part.dtype),
            pltpu.VMEM((rows, width), part.dtype),
            pltpu.SemaphoreType.DMA((pieces,)),
            pltpu.SemaphoreType.DMA((1,)),
            pltpu.SemaphoreType.DMA((1,)),
        ],
        compiler_params=pltpu.CompilerParams(collective_id=1, has_side_effects=True),
    )(part)


def per_device(stored, integrals, layout, partner):
    local_rows = stored.shape[0]
    n_z = lax.axis_size("z")
    n_xh = lax.axis_size("xh")
    n_core = lax.axis_size("core")
    n_row = n_z * n_xh * n_core
    n_col = lax.axis_size(COL_AXES)
    total = local_rows * n_row * n_col
    block = total // n_row

    pieces = stored.reshape(local_rows, n_row, stored.shape[1] // n_row).transpose(1, 0, 2)
    regrouped = exchange_over_row(pieces).reshape(n_row * local_rows, pieces.shape[2])
    gathered = gather_over_col(regrouped, n_col).reshape(total, regrouped.shape[1])

    s = jnp.arange(total, dtype=jnp.int32)
    s_row = s // (local_rows * n_col)
    s_col = (s // local_rows) % n_col
    s_off = s % local_rows
    pos_of_stored = s_col * (n_row * local_rows) + s_row * local_rows + s_off
    inv = _inverse(layout)

    i = jnp.arange(total, dtype=jnp.int32)
    g = i // block
    xh = g % n_xh
    core = (g // n_xh) % n_core
    z = g // (n_xh * n_core)
    p_of_i = ((z * n_xh + xh) * n_core + core) * block + (i % block)
    q = _lookup(partner, p_of_i)

    ladder = jnp.dot(gathered, integrals, preferred_element_type=jnp.float32)
    difference = antisymmetrize(ladder, _lookup(pos_of_stored, _lookup(inv, p_of_i)), _lookup(pos_of_stored, _lookup(inv, q)))
    part = lax.psum_scatter(difference, ("z", "core"), scatter_dimension=0, tiled=True)
    return sum_over_pair(part.reshape(n_xh, block, part.shape[1]))


def solution(mesh):
    n_row, n_col = mesh.devices.shape
    fine = Mesh(mesh.devices.reshape(4, n_row // 8, 2, 2, n_col // 2), ROW_AXES + COL_AXES)
    return jax.shard_map(
        per_device,
        mesh=fine,
        in_specs=(P(ROW_AXES + COL_AXES, None), P(ROW_AXES, COL_AXES), P(), P()),
        out_specs=P(ROW_AXES, COL_AXES),
        check_vma=False,
    )
```

```python
import jax
import jax.numpy as jnp
from jax import lax
from jax.experimental import pallas as pl
from jax.experimental.pallas import tpu as pltpu
from jax.sharding import Mesh, PartitionSpec as P

ROW_AXES = ("z", "xh", "core")
COL_AXES = ("xl", "y")


def _antisym_kernel(own_idx, partner_idx, all_ref, out_ref, own_buf, partner_buf, sem):
    rows = out_ref.shape[0]
    step = pl.program_id(0)
    steps = pl.num_programs(0)

    def issue(at, slot):
        base = at * rows

        def body(r, carry):
            pltpu.make_async_copy(all_ref.at[pl.ds(own_idx[base + r], 1)], own_buf.at[slot, pl.ds(r, 1)], sem.at[0, slot]).start()
            pltpu.make_async_copy(all_ref.at[pl.ds(partner_idx[base + r], 1)], partner_buf.at[slot, pl.ds(r, 1)], sem.at[1, slot]).start()
            return carry

        lax.fori_loop(0, rows, body, 0)

    @pl.when(step == 0)
    def _():
        issue(0, 0)

    @pl.when(step + 1 < steps)
    def _():
        issue(step + 1, (step + 1) % 2)

    slot = step % 2
    pltpu.make_async_copy(all_ref.at[pl.ds(0, rows)], own_buf.at[slot], sem.at[0, slot]).wait()
    pltpu.make_async_copy(all_ref.at[pl.ds(0, rows)], partner_buf.at[slot], sem.at[1, slot]).wait()
    out_ref[...] = own_buf[slot] - partner_buf[slot]


def antisymmetrize(ladder, own_rows, partner_rows, rows=128):
    total, width = ladder.shape
    return pl.pallas_call(
        _antisym_kernel,
        grid_spec=pltpu.PrefetchScalarGridSpec(
            num_scalar_prefetch=2,
            grid=(total // rows,),
            in_specs=[pl.BlockSpec(memory_space=pl.ANY)],
            out_specs=pl.BlockSpec((rows, width), lambda b, own, other: (b, 0)),
            scratch_shapes=[
                pltpu.VMEM((2, rows, width), ladder.dtype),
                pltpu.VMEM((2, rows, width), ladder.dtype),
                pltpu.SemaphoreType.DMA((2, 2)),
            ],
        ),
        out_shape=jax.ShapeDtypeStruct(ladder.shape, ladder.dtype),
        compiler_params=pltpu.CompilerParams(dimension_semantics=("arbitrary",)),
        cost_estimate=pl.CostEstimate(flops=total * width, transcendentals=0, bytes_accessed=3 * total * width * 4),
    )(own_rows, partner_rows, ladder)


def _pair_diff_kernel(a_idx, b_idx, ia_idx, ib_idx, all_ref, out_ref, a_buf, b_buf, o_buf, in_sem, out_sem):
    rows = a_buf.shape[1]
    step = pl.program_id(0)
    steps = pl.num_programs(0)

    def issue(at, slot):
        base = at * rows

        def body(r, carry):
            pltpu.make_async_copy(all_ref.at[pl.ds(a_idx[base + r], 1)], a_buf.at[slot, pl.ds(r, 1)], in_sem.at[0, slot]).start()
            pltpu.make_async_copy(all_ref.at[pl.ds(b_idx[base + r], 1)], b_buf.at[slot, pl.ds(r, 1)], in_sem.at[1, slot]).start()
            return carry

        lax.fori_loop(0, rows, body, 0)

    def drain(slot):
        pltpu.make_async_copy(o_buf.at[slot], out_ref.at[pl.ds(0, 2 * rows)], out_sem.at[slot]).wait()

    @pl.when(step == 0)
    def _():
        issue(0, 0)

    @pl.when(step + 1 < steps)
    def _():
        issue(step + 1, (step + 1) % 2)

    slot = step % 2
    pltpu.make_async_copy(all_ref.at[pl.ds(0, rows)], a_buf.at[slot], in_sem.at[0, slot]).wait()
    pltpu.make_async_copy(all_ref.at[pl.ds(0, rows)], b_buf.at[slot], in_sem.at[1, slot]).wait()

    @pl.when(step >= 2)
    def _():
        drain(slot)

    d = a_buf[slot] - b_buf[slot]
    o_buf[slot, pl.ds(0, rows)] = d
    o_buf[slot, pl.ds(rows, rows)] = -d
    base = step * rows

    def put(r, carry):
        pltpu.make_async_copy(o_buf.at[slot, pl.ds(r, 1)], out_ref.at[pl.ds(ia_idx[base + r], 1)], out_sem.at[slot]).start()
        pltpu.make_async_copy(o_buf.at[slot, pl.ds(rows + r, 1)], out_ref.at[pl.ds(ib_idx[base + r], 1)], out_sem.at[slot]).start()
        return carry

    lax.fori_loop(0, rows, put, 0)

    @pl.when(step == steps - 1)
    def _():
        drain(slot)

        @pl.when(steps >= 2)
        def _():
            drain(1 - slot)


def pair_differences(ladder, a_rows, b_rows, a_out, b_out, rows=64):
    total, width = ladder.shape
    pairs = a_rows.shape[0]
    return pl.pallas_call(
        _pair_diff_kernel,
        grid_spec=pltpu.PrefetchScalarGridSpec(
            num_scalar_prefetch=4,
            grid=(pairs // rows,),
            in_specs=[pl.BlockSpec(memory_space=pl.ANY)],
            out_specs=pl.BlockSpec(memory_space=pl.ANY),
            scratch_shapes=[
                pltpu.VMEM((2, rows, width), ladder.dtype),
                pltpu.VMEM((2, rows, width), ladder.dtype),
                pltpu.VMEM((2, 2 * rows, width), ladder.dtype),
                pltpu.SemaphoreType.DMA((2, 2)),
                pltpu.SemaphoreType.DMA((2,)),
            ],
        ),
        out_shape=jax.ShapeDtypeStruct(ladder.shape, ladder.dtype),
        compiler_params=pltpu.CompilerParams(dimension_semantics=("arbitrary",)),
        cost_estimate=pl.CostEstimate(flops=total * width, transcendentals=0, bytes_accessed=2 * total * width * 4),
    )(a_rows, b_rows, a_out, b_out, ladder)


def _exchange_kernel(src_ref, out_ref, send_sem, recv_sem, local_sem):
    n_z, n_xh, n_core = (lax.axis_size(a) for a in ROW_AXES)
    n = n_z * n_xh * n_core
    z, xh, core, xl, y = (lax.axis_index(a) for a in ROW_AXES + COL_AXES)
    me = (z * n_xh + xh) * n_core + core

    def peer(k):
        t = lax.rem(me + k, n)
        return t, (t // (n_xh * n_core), lax.rem(t // n_core, n_xh), lax.rem(t, n_core), xl, y)

    barrier = pltpu.get_barrier_semaphore()
    for k in range(1, n):
        pl.semaphore_signal(barrier, inc=1, device_id=peer(k)[1], device_id_type=pl.DeviceIdType.MESH)
    pl.semaphore_wait(barrier, n - 1)

    local = pltpu.make_async_copy(src_ref.at[me], out_ref.at[me], local_sem.at[0])
    local.start()
    sends = []
    for k in range(1, n):
        t, where = peer(k)
        copy = pltpu.make_async_remote_copy(
            src_ref=src_ref.at[t],
            dst_ref=out_ref.at[me],
            send_sem=send_sem.at[k - 1],
            recv_sem=recv_sem.at[0],
            device_id=where,
            device_id_type=pl.DeviceIdType.MESH,
        )
        copy.start()
        sends.append(copy)
    for copy in sends:
        copy.wait_send()
    pltpu.make_async_copy(src_ref.at[pl.ds(0, n - 1)], out_ref.at[pl.ds(0, n - 1)], recv_sem.at[0]).wait()
    local.wait()


def exchange_over_row(pieces):
    n = pieces.shape[0]
    return pl.pallas_call(
        _exchange_kernel,
        out_shape=jax.ShapeDtypeStruct(pieces.shape, pieces.dtype),
        in_specs=[pl.BlockSpec(memory_space=pl.ANY)],
        out_specs=pl.BlockSpec(memory_space=pl.ANY),
        scratch_shapes=[
            pltpu.SemaphoreType.DMA((n - 1,)),
            pltpu.SemaphoreType.DMA((1,)),
            pltpu.SemaphoreType.DMA((1,)),
        ],
        compiler_params=pltpu.CompilerParams(collective_id=0, has_side_effects=True),
    )(pieces)


def _pair_sum_kernel(part_ref, out_ref, own_buf, recv_buf, send_sem, recv_sem, local_sem):
    n_xh = lax.axis_size("xh")
    z, xh, core, xl, y = (lax.axis_index(a) for a in ROW_AXES + COL_AXES)
    other = lax.rem(xh + 1, n_xh)
    where = (z, other, core, xl, y)
    pieces = send_sem.shape[0]
    rows = own_buf.shape[0] // pieces

    barrier = pltpu.get_barrier_semaphore()
    pl.semaphore_signal(barrier, inc=1, device_id=where, device_id_type=pl.DeviceIdType.MESH)
    pl.semaphore_wait(barrier, 1)

    local = pltpu.make_async_copy(part_ref.at[xh], own_buf, local_sem.at[0])
    local.start()
    sends = []
    for k in range(pieces):
        copy = pltpu.make_async_remote_copy(
            src_ref=part_ref.at[other, pl.ds(k * rows, rows)],
            dst_ref=recv_buf.at[pl.ds(k * rows, rows)],
            send_sem=send_sem.at[k],
            recv_sem=recv_sem.at[0],
            device_id=where,
            device_id_type=pl.DeviceIdType.MESH,
        )
        copy.start()
        sends.append(copy)
    local.wait()
    for copy in sends:
        copy.wait_send()
    pltpu.make_async_copy(part_ref.at[xh], recv_buf, recv_sem.at[0]).wait()
    out_ref[...] = (own_buf[...] + recv_buf[...]).astype(out_ref.dtype)


def sum_over_pair(part, pieces=4):
    _, rows, width = part.shape
    return pl.pallas_call(
        _pair_sum_kernel,
        out_shape=jax.ShapeDtypeStruct((rows, width), jnp.bfloat16),
        in_specs=[pl.BlockSpec(memory_space=pl.ANY)],
        out_specs=pl.BlockSpec(memory_space=pltpu.VMEM),
        scratch_shapes=[
            pltpu.VMEM((rows, width), part.dtype),
            pltpu.VMEM((rows, width), part.dtype),
            pltpu.SemaphoreType.DMA((pieces,)),
            pltpu.SemaphoreType.DMA((1,)),
            pltpu.SemaphoreType.DMA((1,)),
        ],
        compiler_params=pltpu.CompilerParams(collective_id=1, has_side_effects=True),
    )(part)


def per_device(stored, integrals, layout, partner):
    local_rows = stored.shape[0]
    n_z = lax.axis_size("z")
    n_xh = lax.axis_size("xh")
    n_core = lax.axis_size("core")
    n_row = n_z * n_xh * n_core
    n_col = lax.axis_size(COL_AXES)
    total = local_rows * n_row * n_col
    block = total // n_row

    pieces = stored.reshape(local_rows, n_row, stored.shape[1] // n_row).transpose(1, 0, 2)
    regrouped = exchange_over_row(pieces).reshape(n_row * local_rows, pieces.shape[2])
    gathered = lax.all_gather(regrouped, COL_AXES, axis=0, tiled=True)

    s = jnp.arange(total, dtype=jnp.int32)
    s_row = s // (local_rows * n_col)
    s_col = (s // local_rows) % n_col
    s_off = s % local_rows
    pos_of_stored = s_col * (n_row * local_rows) + s_row * local_rows + s_off
    inv = jnp.zeros((total,), jnp.int32).at[layout].set(s)

    def row_of(p):
        g = p // block
        core = g % n_core
        xh = (g // n_core) % n_xh
        z = g // (n_core * n_xh)
        return ((z * n_core + core) * n_xh + xh) * block + (p % block)

    p_all = jnp.arange(total, dtype=jnp.int32)
    first = partner > p_all
    rank = jnp.cumsum(first.astype(jnp.int32)) - 1
    k = jnp.arange(total // 2, dtype=jnp.int32)
    hits = first[None, :] & (rank[None, :] == k[:, None])
    rep = jnp.sum(jnp.where(hits, p_all[None, :], 0), axis=1)
    other = partner[rep]

    ladder = jnp.dot(gathered, integrals, preferred_element_type=jnp.float32)
    difference = pair_differences(
        ladder, pos_of_stored[inv[rep]], pos_of_stored[inv[other]], row_of(rep), row_of(other)
    )
    part = lax.psum_scatter(difference, ("z", "core"), scatter_dimension=0, tiled=True)
    return sum_over_pair(part.reshape(n_xh, block, part.shape[1]))


def solution(mesh):
    n_row, n_col = mesh.devices.shape
    fine = Mesh(mesh.devices.reshape(4, n_row // 8, 2, 2, n_col // 2), ROW_AXES + COL_AXES)
    return jax.shard_map(
        per_device,
        mesh=fine,
        in_specs=(P(ROW_AXES + COL_AXES, None), P(ROW_AXES, COL_AXES), P(), P()),
        out_specs=P(ROW_AXES, COL_AXES),
        check_vma=False,
    )
```

```python
import jax
import jax.numpy as jnp
from jax import lax
from jax.experimental import pallas as pl
from jax.experimental.pallas import tpu as pltpu
from jax.sharding import Mesh, PartitionSpec as P

ROW_AXES = ("z", "xh", "core")
COL_AXES = ("xl", "y")


def _antisym_kernel(own_idx, partner_idx, all_ref, out_ref, own_buf, partner_buf, sem):
    rows = out_ref.shape[0]
    step = pl.program_id(0)
    steps = pl.num_programs(0)

    def issue(at, slot):
        base = at * rows

        def body(r, carry):
            pltpu.make_async_copy(all_ref.at[pl.ds(own_idx[base + r], 1)], own_buf.at[slot, pl.ds(r, 1)], sem.at[0, slot]).start()
            pltpu.make_async_copy(all_ref.at[pl.ds(partner_idx[base + r], 1)], partner_buf.at[slot, pl.ds(r, 1)], sem.at[1, slot]).start()
            return carry

        lax.fori_loop(0, rows, body, 0)

    @pl.when(step == 0)
    def _():
        issue(0, 0)

    @pl.when(step + 1 < steps)
    def _():
        issue(step + 1, (step + 1) % 2)

    slot = step % 2
    pltpu.make_async_copy(all_ref.at[pl.ds(0, rows)], own_buf.at[slot], sem.at[0, slot]).wait()
    pltpu.make_async_copy(all_ref.at[pl.ds(0, rows)], partner_buf.at[slot], sem.at[1, slot]).wait()
    out_ref[...] = own_buf[slot] - partner_buf[slot]


def antisymmetrize(ladder, own_rows, partner_rows, rows=128):
    total, width = ladder.shape
    return pl.pallas_call(
        _antisym_kernel,
        grid_spec=pltpu.PrefetchScalarGridSpec(
            num_scalar_prefetch=2,
            grid=(total // rows,),
            in_specs=[pl.BlockSpec(memory_space=pl.ANY)],
            out_specs=pl.BlockSpec((rows, width), lambda b, own, other: (b, 0)),
            scratch_shapes=[
                pltpu.VMEM((2, rows, width), ladder.dtype),
                pltpu.VMEM((2, rows, width), ladder.dtype),
                pltpu.SemaphoreType.DMA((2, 2)),
            ],
        ),
        out_shape=jax.ShapeDtypeStruct(ladder.shape, ladder.dtype),
        compiler_params=pltpu.CompilerParams(dimension_semantics=("arbitrary",)),
        cost_estimate=pl.CostEstimate(flops=total * width, transcendentals=0, bytes_accessed=3 * total * width * 4),
    )(own_rows, partner_rows, ladder)


def _pair_diff_kernel(a_idx, b_idx, ia_idx, ib_idx, all_ref, out_ref, a_buf, b_buf, o_buf, in_sem, out_sem):
    rows = a_buf.shape[1]
    step = pl.program_id(0)
    steps = pl.num_programs(0)

    def issue(at, slot):
        base = at * rows

        def body(r, carry):
            pltpu.make_async_copy(all_ref.at[pl.ds(a_idx[base + r], 1)], a_buf.at[slot, pl.ds(r, 1)], in_sem.at[0, slot]).start()
            pltpu.make_async_copy(all_ref.at[pl.ds(b_idx[base + r], 1)], b_buf.at[slot, pl.ds(r, 1)], in_sem.at[1, slot]).start()
            return carry

        lax.fori_loop(0, rows, body, 0)

    def drain(slot):
        pltpu.make_async_copy(o_buf.at[slot], out_ref.at[pl.ds(0, 2 * rows)], out_sem.at[slot]).wait()

    @pl.when(step == 0)
    def _():
        issue(0, 0)

    @pl.when(step + 1 < steps)
    def _():
        issue(step + 1, (step + 1) % 2)

    slot = step % 2
    pltpu.make_async_copy(all_ref.at[pl.ds(0, rows)], a_buf.at[slot], in_sem.at[0, slot]).wait()
    pltpu.make_async_copy(all_ref.at[pl.ds(0, rows)], b_buf.at[slot], in_sem.at[1, slot]).wait()

    @pl.when(step >= 2)
    def _():
        drain(slot)

    d = a_buf[slot] - b_buf[slot]
    o_buf[slot, pl.ds(0, rows)] = d
    o_buf[slot, pl.ds(rows, rows)] = -d
    base = step * rows

    def put(r, carry):
        pltpu.make_async_copy(o_buf.at[slot, pl.ds(r, 1)], out_ref.at[pl.ds(ia_idx[base + r], 1)], out_sem.at[slot]).start()
        pltpu.make_async_copy(o_buf.at[slot, pl.ds(rows + r, 1)], out_ref.at[pl.ds(ib_idx[base + r], 1)], out_sem.at[slot]).start()
        return carry

    lax.fori_loop(0, rows, put, 0)

    @pl.when(step == steps - 1)
    def _():
        drain(slot)

        @pl.when(steps >= 2)
        def _():
            drain(1 - slot)


def pair_differences(ladder, a_rows, b_rows, a_out, b_out, rows=64):
    total, width = ladder.shape
    pairs = a_rows.shape[0]
    return pl.pallas_call(
        _pair_diff_kernel,
        grid_spec=pltpu.PrefetchScalarGridSpec(
            num_scalar_prefetch=4,
            grid=(pairs // rows,),
            in_specs=[pl.BlockSpec(memory_space=pl.ANY)],
            out_specs=pl.BlockSpec(memory_space=pl.ANY),
            scratch_shapes=[
                pltpu.VMEM((2, rows, width), ladder.dtype),
                pltpu.VMEM((2, rows, width), ladder.dtype),
                pltpu.VMEM((2, 2 * rows, width), ladder.dtype),
                pltpu.SemaphoreType.DMA((2, 2)),
                pltpu.SemaphoreType.DMA((2,)),
            ],
        ),
        out_shape=jax.ShapeDtypeStruct(ladder.shape, ladder.dtype),
        compiler_params=pltpu.CompilerParams(dimension_semantics=("arbitrary",)),
        cost_estimate=pl.CostEstimate(flops=total * width, transcendentals=0, bytes_accessed=2 * total * width * 4),
    )(a_rows, b_rows, a_out, b_out, ladder)


def _exchange_kernel(src_ref, out_ref, send_sem, recv_sem, local_sem):
    n_z, n_xh, n_core = (lax.axis_size(a) for a in ROW_AXES)
    n = n_z * n_xh * n_core
    z, xh, core, xl, y = (lax.axis_index(a) for a in ROW_AXES + COL_AXES)
    me = (z * n_xh + xh) * n_core + core

    def peer(k):
        t = lax.rem(me + k, n)
        return t, (t // (n_xh * n_core), lax.rem(t // n_core, n_xh), lax.rem(t, n_core), xl, y)

    barrier = pltpu.get_barrier_semaphore()
    for k in range(1, n):
        pl.semaphore_signal(barrier, inc=1, device_id=peer(k)[1], device_id_type=pl.DeviceIdType.MESH)
    pl.semaphore_wait(barrier, n - 1)

    local = pltpu.make_async_copy(src_ref.at[me], out_ref.at[me], local_sem.at[0])
    local.start()
    sends = []
    for k in range(1, n):
        t, where = peer(k)
        copy = pltpu.make_async_remote_copy(
            src_ref=src_ref.at[t],
            dst_ref=out_ref.at[me],
            send_sem=send_sem.at[k - 1],
            recv_sem=recv_sem.at[0],
            device_id=where,
            device_id_type=pl.DeviceIdType.MESH,
        )
        copy.start()
        sends.append(copy)
    for copy in sends:
        copy.wait_send()
    pltpu.make_async_copy(src_ref.at[pl.ds(0, n - 1)], out_ref.at[pl.ds(0, n - 1)], recv_sem.at[0]).wait()
    local.wait()


def exchange_over_row(pieces):
    n = pieces.shape[0]
    return pl.pallas_call(
        _exchange_kernel,
        out_shape=jax.ShapeDtypeStruct(pieces.shape, pieces.dtype),
        in_specs=[pl.BlockSpec(memory_space=pl.ANY)],
        out_specs=pl.BlockSpec(memory_space=pl.ANY),
        scratch_shapes=[
            pltpu.SemaphoreType.DMA((n - 1,)),
            pltpu.SemaphoreType.DMA((1,)),
            pltpu.SemaphoreType.DMA((1,)),
        ],
        compiler_params=pltpu.CompilerParams(collective_id=0, has_side_effects=True),
    )(pieces)


def _pair_sum_kernel(part_ref, out_ref, own_buf, recv_buf, send_sem, recv_sem, local_sem):
    n_xh = lax.axis_size("xh")
    z, xh, core, xl, y = (lax.axis_index(a) for a in ROW_AXES + COL_AXES)
    other = lax.rem(xh + 1, n_xh)
    where = (z, other, core, xl, y)
    pieces = send_sem.shape[0]
    rows = own_buf.shape[0] // pieces

    barrier = pltpu.get_barrier_semaphore()
    pl.semaphore_signal(barrier, inc=1, device_id=where, device_id_type=pl.DeviceIdType.MESH)
    pl.semaphore_wait(barrier, 1)

    local = pltpu.make_async_copy(part_ref.at[xh], own_buf, local_sem.at[0])
    local.start()
    sends = []
    for k in range(pieces):
        copy = pltpu.make_async_remote_copy(
            src_ref=part_ref.at[other, pl.ds(k * rows, rows)],
            dst_ref=recv_buf.at[pl.ds(k * rows, rows)],
            send_sem=send_sem.at[k],
            recv_sem=recv_sem.at[0],
            device_id=where,
            device_id_type=pl.DeviceIdType.MESH,
        )
        copy.start()
        sends.append(copy)
    local.wait()
    for copy in sends:
        copy.wait_send()
    pltpu.make_async_copy(part_ref.at[xh], recv_buf, recv_sem.at[0]).wait()
    out_ref[...] = (own_buf[...] + recv_buf[...]).astype(out_ref.dtype)


def sum_over_pair(part, pieces=4):
    _, rows, width = part.shape
    return pl.pallas_call(
        _pair_sum_kernel,
        out_shape=jax.ShapeDtypeStruct((rows, width), jnp.bfloat16),
        in_specs=[pl.BlockSpec(memory_space=pl.ANY)],
        out_specs=pl.BlockSpec(memory_space=pltpu.VMEM),
        scratch_shapes=[
            pltpu.VMEM((rows, width), part.dtype),
            pltpu.VMEM((rows, width), part.dtype),
            pltpu.SemaphoreType.DMA((pieces,)),
            pltpu.SemaphoreType.DMA((1,)),
            pltpu.SemaphoreType.DMA((1,)),
        ],
        compiler_params=pltpu.CompilerParams(collective_id=1, has_side_effects=True),
    )(part)


def per_device(stored, integrals, layout, partner):
    local_rows = stored.shape[0]
    n_z = lax.axis_size("z")
    n_xh = lax.axis_size("xh")
    n_core = lax.axis_size("core")
    n_row = n_z * n_xh * n_core
    n_col = lax.axis_size(COL_AXES)
    total = local_rows * n_row * n_col
    block = total // n_row

    pieces = stored.reshape(local_rows, n_row, stored.shape[1] // n_row).transpose(1, 0, 2)
    regrouped = exchange_over_row(pieces).reshape(n_row * local_rows, pieces.shape[2])
    gathered = lax.all_gather(regrouped, COL_AXES, axis=0, tiled=True)

    s = jnp.arange(total, dtype=jnp.int32)
    s_row = s // (local_rows * n_col)
    s_col = (s // local_rows) % n_col
    s_off = s % local_rows
    pos_of_stored = s_col * (n_row * local_rows) + s_row * local_rows + s_off
    inv = jnp.zeros((total,), jnp.int32).at[layout].set(s)

    def row_of(p):
        g = p // block
        core = g % n_core
        xh = (g // n_core) % n_xh
        z = g // (n_core * n_xh)
        return ((z * n_core + core) * n_xh + xh) * block + (p % block)

    p_all = jnp.arange(total, dtype=jnp.int32)
    first = partner > p_all
    rank = jnp.cumsum(first.astype(jnp.int32)) - 1
    k = jnp.arange(total // 2, dtype=jnp.int32)
    hits = first[None, :] & (rank[None, :] == k[:, None])
    rep = jnp.sum(jnp.where(hits, p_all[None, :], 0), axis=1)
    other = partner[rep]

    ladder = jnp.dot(gathered, integrals, preferred_element_type=jnp.float32)
    difference = pair_differences(
        ladder, pos_of_stored[inv[rep]], pos_of_stored[inv[other]], row_of(rep), row_of(other)
    )
    part = lax.psum_scatter(difference, ("z", "core"), scatter_dimension=0, tiled=True)
    halves = part.reshape(n_xh, block, part.shape[1])
    xh_me = lax.axis_index("xh")
    mine = lax.dynamic_index_in_dim(halves, xh_me, keepdims=False)
    theirs = lax.dynamic_index_in_dim(halves, lax.rem(xh_me + 1, n_xh), keepdims=False)
    received = lax.ppermute(theirs, "xh", perm=[(j, (j + 1) % n_xh) for j in range(n_xh)])
    return (mine + received).astype(jnp.bfloat16)


def solution(mesh):
    n_row, n_col = mesh.devices.shape
    fine = Mesh(mesh.devices.reshape(4, n_row // 8, 2, 2, n_col // 2), ROW_AXES + COL_AXES)
    return jax.shard_map(
        per_device,
        mesh=fine,
        in_specs=(P(ROW_AXES + COL_AXES, None), P(ROW_AXES, COL_AXES), P(), P()),
        out_specs=P(ROW_AXES, COL_AXES),
        check_vma=False,
    )
```

```python
import jax
import jax.numpy as jnp
from jax import lax
from jax.experimental import pallas as pl
from jax.experimental.pallas import tpu as pltpu
from jax.sharding import Mesh, PartitionSpec as P

ROW_AXES = ("z", "xh", "core")
COL_AXES = ("xl", "y")


def _antisym_kernel(own_idx, partner_idx, all_ref, out_ref, own_buf, partner_buf, sem):
    rows = out_ref.shape[0]
    step = pl.program_id(0)
    steps = pl.num_programs(0)

    def issue(at, slot):
        base = at * rows

        def body(r, carry):
            pltpu.make_async_copy(all_ref.at[pl.ds(own_idx[base + r], 1)], own_buf.at[slot, pl.ds(r, 1)], sem.at[0, slot]).start()
            pltpu.make_async_copy(all_ref.at[pl.ds(partner_idx[base + r], 1)], partner_buf.at[slot, pl.ds(r, 1)], sem.at[1, slot]).start()
            return carry

        lax.fori_loop(0, rows, body, 0)

    @pl.when(step == 0)
    def _():
        issue(0, 0)

    @pl.when(step + 1 < steps)
    def _():
        issue(step + 1, (step + 1) % 2)

    slot = step % 2
    pltpu.make_async_copy(all_ref.at[pl.ds(0, rows)], own_buf.at[slot], sem.at[0, slot]).wait()
    pltpu.make_async_copy(all_ref.at[pl.ds(0, rows)], partner_buf.at[slot], sem.at[1, slot]).wait()
    out_ref[...] = own_buf[slot] - partner_buf[slot]


def antisymmetrize(ladder, own_rows, partner_rows, rows=128):
    total, width = ladder.shape
    return pl.pallas_call(
        _antisym_kernel,
        grid_spec=pltpu.PrefetchScalarGridSpec(
            num_scalar_prefetch=2,
            grid=(total // rows,),
            in_specs=[pl.BlockSpec(memory_space=pl.ANY)],
            out_specs=pl.BlockSpec((rows, width), lambda b, own, other: (b, 0)),
            scratch_shapes=[
                pltpu.VMEM((2, rows, width), ladder.dtype),
                pltpu.VMEM((2, rows, width), ladder.dtype),
                pltpu.SemaphoreType.DMA((2, 2)),
            ],
        ),
        out_shape=jax.ShapeDtypeStruct(ladder.shape, ladder.dtype),
        compiler_params=pltpu.CompilerParams(dimension_semantics=("arbitrary",)),
        cost_estimate=pl.CostEstimate(flops=total * width, transcendentals=0, bytes_accessed=3 * total * width * 4),
    )(own_rows, partner_rows, ladder)


def _pair_diff_kernel(a_idx, b_idx, ia_idx, ib_idx, all_ref, out_ref, a_buf, b_buf, o_buf, in_sem, out_sem):
    rows = a_buf.shape[1]
    step = pl.program_id(0)
    steps = pl.num_programs(0)

    def issue(at, slot):
        base = at * rows

        def body(r, carry):
            pltpu.make_async_copy(all_ref.at[pl.ds(a_idx[base + r], 1)], a_buf.at[slot, pl.ds(r, 1)], in_sem.at[0, slot]).start()
            pltpu.make_async_copy(all_ref.at[pl.ds(b_idx[base + r], 1)], b_buf.at[slot, pl.ds(r, 1)], in_sem.at[1, slot]).start()
            return carry

        lax.fori_loop(0, rows, body, 0)

    def drain(slot):
        pltpu.make_async_copy(o_buf.at[slot], out_ref.at[pl.ds(0, 2 * rows)], out_sem.at[slot]).wait()

    @pl.when(step == 0)
    def _():
        issue(0, 0)

    @pl.when(step + 1 < steps)
    def _():
        issue(step + 1, (step + 1) % 2)

    slot = step % 2
    pltpu.make_async_copy(all_ref.at[pl.ds(0, rows)], a_buf.at[slot], in_sem.at[0, slot]).wait()
    pltpu.make_async_copy(all_ref.at[pl.ds(0, rows)], b_buf.at[slot], in_sem.at[1, slot]).wait()

    @pl.when(step >= 2)
    def _():
        drain(slot)

    d = a_buf[slot] - b_buf[slot]
    o_buf[slot, pl.ds(0, rows)] = d
    o_buf[slot, pl.ds(rows, rows)] = -d
    base = step * rows

    def put(r, carry):
        pltpu.make_async_copy(o_buf.at[slot, pl.ds(r, 1)], out_ref.at[pl.ds(ia_idx[base + r], 1)], out_sem.at[slot]).start()
        pltpu.make_async_copy(o_buf.at[slot, pl.ds(rows + r, 1)], out_ref.at[pl.ds(ib_idx[base + r], 1)], out_sem.at[slot]).start()
        return carry

    lax.fori_loop(0, rows, put, 0)

    @pl.when(step == steps - 1)
    def _():
        drain(slot)

        @pl.when(steps >= 2)
        def _():
            drain(1 - slot)


def pair_differences(ladder, a_rows, b_rows, a_out, b_out, rows=128):
    total, width = ladder.shape
    pairs = a_rows.shape[0]
    return pl.pallas_call(
        _pair_diff_kernel,
        grid_spec=pltpu.PrefetchScalarGridSpec(
            num_scalar_prefetch=4,
            grid=(pairs // rows,),
            in_specs=[pl.BlockSpec(memory_space=pl.ANY)],
            out_specs=pl.BlockSpec(memory_space=pl.ANY),
            scratch_shapes=[
                pltpu.VMEM((2, rows, width), ladder.dtype),
                pltpu.VMEM((2, rows, width), ladder.dtype),
                pltpu.VMEM((2, 2 * rows, width), ladder.dtype),
                pltpu.SemaphoreType.DMA((2, 2)),
                pltpu.SemaphoreType.DMA((2,)),
            ],
        ),
        out_shape=jax.ShapeDtypeStruct(ladder.shape, ladder.dtype),
        compiler_params=pltpu.CompilerParams(dimension_semantics=("arbitrary",)),
        cost_estimate=pl.CostEstimate(flops=total * width, transcendentals=0, bytes_accessed=2 * total * width * 4),
    )(a_rows, b_rows, a_out, b_out, ladder)


def _exchange_kernel(src_ref, out_ref, send_sem, recv_sem, local_sem):
    n_z, n_xh, n_core = (lax.axis_size(a) for a in ROW_AXES)
    n = n_z * n_xh * n_core
    z, xh, core, xl, y = (lax.axis_index(a) for a in ROW_AXES + COL_AXES)
    me = (z * n_xh + xh) * n_core + core

    def peer(k):
        t = lax.rem(me + k, n)
        return t, (t // (n_xh * n_core), lax.rem(t // n_core, n_xh), lax.rem(t, n_core), xl, y)

    barrier = pltpu.get_barrier_semaphore()
    for k in range(1, n):
        pl.semaphore_signal(barrier, inc=1, device_id=peer(k)[1], device_id_type=pl.DeviceIdType.MESH)
    pl.semaphore_wait(barrier, n - 1)

    local = pltpu.make_async_copy(src_ref.at[me], out_ref.at[me], local_sem.at[0])
    local.start()
    sends = []
    for k in range(1, n):
        t, where = peer(k)
        copy = pltpu.make_async_remote_copy(
            src_ref=src_ref.at[t],
            dst_ref=out_ref.at[me],
            send_sem=send_sem.at[k - 1],
            recv_sem=recv_sem.at[0],
            device_id=where,
            device_id_type=pl.DeviceIdType.MESH,
        )
        copy.start()
        sends.append(copy)
    for copy in sends:
        copy.wait_send()
    pltpu.make_async_copy(src_ref.at[pl.ds(0, n - 1)], out_ref.at[pl.ds(0, n - 1)], recv_sem.at[0]).wait()
    local.wait()


def exchange_over_row(pieces):
    n = pieces.shape[0]
    return pl.pallas_call(
        _exchange_kernel,
        out_shape=jax.ShapeDtypeStruct(pieces.shape, pieces.dtype),
        in_specs=[pl.BlockSpec(memory_space=pl.ANY)],
        out_specs=pl.BlockSpec(memory_space=pl.ANY),
        scratch_shapes=[
            pltpu.SemaphoreType.DMA((n - 1,)),
            pltpu.SemaphoreType.DMA((1,)),
            pltpu.SemaphoreType.DMA((1,)),
        ],
        compiler_params=pltpu.CompilerParams(collective_id=0, has_side_effects=True),
    )(pieces)


def _pair_sum_kernel(part_ref, out_ref, own_buf, recv_buf, send_sem, recv_sem, local_sem):
    n_xh = lax.axis_size("xh")
    z, xh, core, xl, y = (lax.axis_index(a) for a in ROW_AXES + COL_AXES)
    other = lax.rem(xh + 1, n_xh)
    where = (z, other, core, xl, y)
    pieces = send_sem.shape[0]
    rows = own_buf.shape[0] // pieces

    barrier = pltpu.get_barrier_semaphore()
    pl.semaphore_signal(barrier, inc=1, device_id=where, device_id_type=pl.DeviceIdType.MESH)
    pl.semaphore_wait(barrier, 1)

    local = pltpu.make_async_copy(part_ref.at[xh], own_buf, local_sem.at[0])
    local.start()
    sends = []
    for k in range(pieces):
        copy = pltpu.make_async_remote_copy(
            src_ref=part_ref.at[other, pl.ds(k * rows, rows)],
            dst_ref=recv_buf.at[pl.ds(k * rows, rows)],
            send_sem=send_sem.at[k],
            recv_sem=recv_sem.at[0],
            device_id=where,
            device_id_type=pl.DeviceIdType.MESH,
        )
        copy.start()
        sends.append(copy)
    local.wait()
    for copy in sends:
        copy.wait_send()
    pltpu.make_async_copy(part_ref.at[xh], recv_buf, recv_sem.at[0]).wait()
    out_ref[...] = (own_buf[...] + recv_buf[...]).astype(out_ref.dtype)


def sum_over_pair(part, pieces=4):
    _, rows, width = part.shape
    return pl.pallas_call(
        _pair_sum_kernel,
        out_shape=jax.ShapeDtypeStruct((rows, width), jnp.bfloat16),
        in_specs=[pl.BlockSpec(memory_space=pl.ANY)],
        out_specs=pl.BlockSpec(memory_space=pltpu.VMEM),
        scratch_shapes=[
            pltpu.VMEM((rows, width), part.dtype),
            pltpu.VMEM((rows, width), part.dtype),
            pltpu.SemaphoreType.DMA((pieces,)),
            pltpu.SemaphoreType.DMA((1,)),
            pltpu.SemaphoreType.DMA((1,)),
        ],
        compiler_params=pltpu.CompilerParams(collective_id=1, has_side_effects=True),
    )(part)


def per_device(stored, integrals, layout, partner):
    local_rows = stored.shape[0]
    n_z = lax.axis_size("z")
    n_xh = lax.axis_size("xh")
    n_core = lax.axis_size("core")
    n_row = n_z * n_xh * n_core
    n_col = lax.axis_size(COL_AXES)
    total = local_rows * n_row * n_col
    block = total // n_row

    pieces = stored.reshape(local_rows, n_row, stored.shape[1] // n_row).transpose(1, 0, 2)
    regrouped = exchange_over_row(pieces).reshape(n_row * local_rows, pieces.shape[2])
    gathered = lax.all_gather(regrouped, COL_AXES, axis=0, tiled=True)

    s = jnp.arange(total, dtype=jnp.int32)
    s_row = s // (local_rows * n_col)
    s_col = (s // local_rows) % n_col
    s_off = s % local_rows
    pos_of_stored = s_col * (n_row * local_rows) + s_row * local_rows + s_off
    inv = jnp.zeros((total,), jnp.int32).at[layout].set(s)

    def row_of(p):
        g = p // block
        core = g % n_core
        xh = (g // n_core) % n_xh
        z = g // (n_core * n_xh)
        return ((z * n_core + core) * n_xh + xh) * block + (p % block)

    p_all = jnp.arange(total, dtype=jnp.int32)
    first = partner > p_all
    rank = jnp.cumsum(first.astype(jnp.int32)) - 1
    k = jnp.arange(total // 2, dtype=jnp.int32)
    hits = first[None, :] & (rank[None, :] == k[:, None])
    rep = jnp.sum(jnp.where(hits, p_all[None, :], 0), axis=1)
    other = partner[rep]

    ladder = jnp.dot(gathered, integrals, preferred_element_type=jnp.float32)
    difference = pair_differences(
        ladder, pos_of_stored[inv[rep]], pos_of_stored[inv[other]], row_of(rep), row_of(other)
    )
    part = lax.psum_scatter(difference, ("z", "core"), scatter_dimension=0, tiled=True)
    return sum_over_pair(part.reshape(n_xh, block, part.shape[1]))


def solution(mesh):
    n_row, n_col = mesh.devices.shape
    fine = Mesh(mesh.devices.reshape(4, n_row // 8, 2, 2, n_col // 2), ROW_AXES + COL_AXES)
    return jax.shard_map(
        per_device,
        mesh=fine,
        in_specs=(P(ROW_AXES + COL_AXES, None), P(ROW_AXES, COL_AXES), P(), P()),
        out_specs=P(ROW_AXES, COL_AXES),
        check_vma=False,
    )
```

```python
import jax
import jax.numpy as jnp
from jax import lax
from jax.experimental import pallas as pl
from jax.experimental.pallas import tpu as pltpu
from jax.sharding import Mesh, PartitionSpec as P

ROW_AXES = ("z", "xh", "core")
COL_AXES = ("xl", "y")


def _antisym_kernel(own_idx, partner_idx, all_ref, out_ref, own_buf, partner_buf, sem):
    rows = out_ref.shape[0]
    step = pl.program_id(0)
    steps = pl.num_programs(0)

    def issue(at, slot):
        base = at * rows

        def body(r, carry):
            pltpu.make_async_copy(all_ref.at[pl.ds(own_idx[base + r], 1)], own_buf.at[slot, pl.ds(r, 1)], sem.at[0, slot]).start()
            pltpu.make_async_copy(all_ref.at[pl.ds(partner_idx[base + r], 1)], partner_buf.at[slot, pl.ds(r, 1)], sem.at[1, slot]).start()
            return carry

        lax.fori_loop(0, rows, body, 0)

    @pl.when(step == 0)
    def _():
        issue(0, 0)

    @pl.when(step + 1 < steps)
    def _():
        issue(step + 1, (step + 1) % 2)

    slot = step % 2
    pltpu.make_async_copy(all_ref.at[pl.ds(0, rows)], own_buf.at[slot], sem.at[0, slot]).wait()
    pltpu.make_async_copy(all_ref.at[pl.ds(0, rows)], partner_buf.at[slot], sem.at[1, slot]).wait()
    out_ref[...] = own_buf[slot] - partner_buf[slot]


def antisymmetrize(ladder, own_rows, partner_rows, rows=128):
    total, width = ladder.shape
    return pl.pallas_call(
        _antisym_kernel,
        grid_spec=pltpu.PrefetchScalarGridSpec(
            num_scalar_prefetch=2,
            grid=(total // rows,),
            in_specs=[pl.BlockSpec(memory_space=pl.ANY)],
            out_specs=pl.BlockSpec((rows, width), lambda b, own, other: (b, 0)),
            scratch_shapes=[
                pltpu.VMEM((2, rows, width), ladder.dtype),
                pltpu.VMEM((2, rows, width), ladder.dtype),
                pltpu.SemaphoreType.DMA((2, 2)),
            ],
        ),
        out_shape=jax.ShapeDtypeStruct(ladder.shape, ladder.dtype),
        compiler_params=pltpu.CompilerParams(dimension_semantics=("arbitrary",)),
        cost_estimate=pl.CostEstimate(flops=total * width, transcendentals=0, bytes_accessed=3 * total * width * 4),
    )(own_rows, partner_rows, ladder)


def _pair_diff_kernel(a_idx, b_idx, ia_idx, ib_idx, all_ref, out_ref, a_buf, b_buf, o_buf, in_sem, out_sem):
    rows = a_buf.shape[1]
    step = pl.program_id(0)
    steps = pl.num_programs(0)

    def issue(at, slot):
        base = at * rows

        def body(r, carry):
            pltpu.make_async_copy(all_ref.at[pl.ds(a_idx[base + r], 1)], a_buf.at[slot, pl.ds(r, 1)], in_sem.at[0, slot]).start()
            pltpu.make_async_copy(all_ref.at[pl.ds(b_idx[base + r], 1)], b_buf.at[slot, pl.ds(r, 1)], in_sem.at[1, slot]).start()
            return carry

        lax.fori_loop(0, rows, body, 0)

    def drain(slot):
        pltpu.make_async_copy(o_buf.at[slot], out_ref.at[pl.ds(0, 2 * rows)], out_sem.at[slot]).wait()

    @pl.when(step == 0)
    def _():
        issue(0, 0)

    @pl.when(step + 1 < steps)
    def _():
        issue(step + 1, (step + 1) % 2)

    slot = step % 2
    pltpu.make_async_copy(all_ref.at[pl.ds(0, rows)], a_buf.at[slot], in_sem.at[0, slot]).wait()
    pltpu.make_async_copy(all_ref.at[pl.ds(0, rows)], b_buf.at[slot], in_sem.at[1, slot]).wait()

    @pl.when(step >= 2)
    def _():
        drain(slot)

    d = a_buf[slot] - b_buf[slot]
    o_buf[slot, pl.ds(0, rows)] = d
    o_buf[slot, pl.ds(rows, rows)] = -d
    base = step * rows

    def put(r, carry):
        pltpu.make_async_copy(o_buf.at[slot, pl.ds(r, 1)], out_ref.at[pl.ds(ia_idx[base + r], 1)], out_sem.at[slot]).start()
        pltpu.make_async_copy(o_buf.at[slot, pl.ds(rows + r, 1)], out_ref.at[pl.ds(ib_idx[base + r], 1)], out_sem.at[slot]).start()
        return carry

    lax.fori_loop(0, rows, put, 0)

    @pl.when(step == steps - 1)
    def _():
        drain(slot)

        @pl.when(steps >= 2)
        def _():
            drain(1 - slot)


def pair_differences(ladder, a_rows, b_rows, a_out, b_out, rows=64):
    total, width = ladder.shape
    pairs = a_rows.shape[0]
    return pl.pallas_call(
        _pair_diff_kernel,
        grid_spec=pltpu.PrefetchScalarGridSpec(
            num_scalar_prefetch=4,
            grid=(pairs // rows,),
            in_specs=[pl.BlockSpec(memory_space=pl.ANY)],
            out_specs=pl.BlockSpec(memory_space=pl.ANY),
            scratch_shapes=[
                pltpu.VMEM((2, rows, width), ladder.dtype),
                pltpu.VMEM((2, rows, width), ladder.dtype),
                pltpu.VMEM((2, 2 * rows, width), ladder.dtype),
                pltpu.SemaphoreType.DMA((2, 2)),
                pltpu.SemaphoreType.DMA((2,)),
            ],
        ),
        out_shape=jax.ShapeDtypeStruct(ladder.shape, ladder.dtype),
        compiler_params=pltpu.CompilerParams(dimension_semantics=("arbitrary",)),
        cost_estimate=pl.CostEstimate(flops=total * width, transcendentals=0, bytes_accessed=2 * total * width * 4),
    )(a_rows, b_rows, a_out, b_out, ladder)


def _exchange_kernel(src_ref, out_ref, send_sem, recv_sem, local_sem):
    n_z, n_xh, n_core = (lax.axis_size(a) for a in ROW_AXES)
    n = n_z * n_xh * n_core
    z, xh, core, xl, y = (lax.axis_index(a) for a in ROW_AXES + COL_AXES)
    me = (z * n_xh + xh) * n_core + core

    def peer(k):
        t = lax.rem(me + k, n)
        return t, (t // (n_xh * n_core), lax.rem(t // n_core, n_xh), lax.rem(t, n_core), xl, y)

    barrier = pltpu.get_barrier_semaphore()
    for k in range(1, n):
        pl.semaphore_signal(barrier, inc=1, device_id=peer(k)[1], device_id_type=pl.DeviceIdType.MESH)
    pl.semaphore_wait(barrier, n - 1)

    local = pltpu.make_async_copy(src_ref.at[me], out_ref.at[me], local_sem.at[0])
    local.start()
    sends = []
    for k in range(1, n):
        t, where = peer(k)
        copy = pltpu.make_async_remote_copy(
            src_ref=src_ref.at[t],
            dst_ref=out_ref.at[me],
            send_sem=send_sem.at[k - 1],
            recv_sem=recv_sem.at[0],
            device_id=where,
            device_id_type=pl.DeviceIdType.MESH,
        )
        copy.start()
        sends.append(copy)
    for copy in sends:
        copy.wait_send()
    pltpu.make_async_copy(src_ref.at[pl.ds(0, n - 1)], out_ref.at[pl.ds(0, n - 1)], recv_sem.at[0]).wait()
    local.wait()


def exchange_over_row(pieces):
    n = pieces.shape[0]
    return pl.pallas_call(
        _exchange_kernel,
        out_shape=jax.ShapeDtypeStruct(pieces.shape, pieces.dtype),
        in_specs=[pl.BlockSpec(memory_space=pl.ANY)],
        out_specs=pl.BlockSpec(memory_space=pl.ANY),
        scratch_shapes=[
            pltpu.SemaphoreType.DMA((n - 1,)),
            pltpu.SemaphoreType.DMA((1,)),
            pltpu.SemaphoreType.DMA((1,)),
        ],
        compiler_params=pltpu.CompilerParams(collective_id=0, has_side_effects=True),
    )(pieces)


def _pair_sum_kernel(part_ref, out_ref, own_buf, recv_buf, res_buf, send_sem, recv_sem, local_sem):
    n_xh = lax.axis_size("xh")
    z, xh, core, xl, y = (lax.axis_index(a) for a in ROW_AXES + COL_AXES)
    other = lax.rem(xh + 1, n_xh)
    where = (z, other, core, xl, y)
    pieces = send_sem.shape[0]
    rows = own_buf.shape[0] // pieces

    barrier = pltpu.get_barrier_semaphore()
    pl.semaphore_signal(barrier, inc=1, device_id=where, device_id_type=pl.DeviceIdType.MESH)
    pl.semaphore_wait(barrier, 1)

    local = pltpu.make_async_copy(part_ref.at[xh], own_buf, local_sem.at[0])
    local.start()
    sends = []
    for k in range(pieces):
        copy = pltpu.make_async_remote_copy(
            src_ref=part_ref.at[other, pl.ds(k * rows, rows)],
            dst_ref=recv_buf.at[pl.ds(k * rows, rows)],
            send_sem=send_sem.at[k],
            recv_sem=recv_sem.at[0],
            device_id=where,
            device_id_type=pl.DeviceIdType.MESH,
        )
        copy.start()
        sends.append(copy)
    local.wait()
    for copy in sends:
        copy.wait_send()
    pltpu.make_async_copy(part_ref.at[xh], recv_buf, recv_sem.at[0]).wait()
    res_buf[...] = (own_buf[...] + recv_buf[...]).astype(res_buf.dtype)
    result = pltpu.make_async_copy(res_buf, out_ref, local_sem.at[0])
    result.start()
    result.wait()


def sum_over_pair(part, pieces=4):
    _, rows, width = part.shape
    return pl.pallas_call(
        _pair_sum_kernel,
        out_shape=jax.ShapeDtypeStruct((rows, width), jnp.bfloat16),
        in_specs=[pl.BlockSpec(memory_space=pl.ANY)],
        out_specs=pl.BlockSpec(memory_space=pl.ANY),
        scratch_shapes=[
            pltpu.VMEM((rows, width), part.dtype),
            pltpu.VMEM((rows, width), part.dtype),
            pltpu.VMEM((rows, width), jnp.bfloat16),
            pltpu.SemaphoreType.DMA((pieces,)),
            pltpu.SemaphoreType.DMA((1,)),
            pltpu.SemaphoreType.DMA((1,)),
        ],
        compiler_params=pltpu.CompilerParams(collective_id=1, has_side_effects=True),
    )(part)


def per_device(stored, integrals, layout, partner):
    local_rows = stored.shape[0]
    n_z = lax.axis_size("z")
    n_xh = lax.axis_size("xh")
    n_core = lax.axis_size("core")
    n_row = n_z * n_xh * n_core
    n_col = lax.axis_size(COL_AXES)
    total = local_rows * n_row * n_col
    block = total // n_row

    pieces = stored.reshape(local_rows, n_row, stored.shape[1] // n_row).transpose(1, 0, 2)
    regrouped = exchange_over_row(pieces).reshape(n_row * local_rows, pieces.shape[2])
    gathered = lax.all_gather(regrouped, COL_AXES, axis=0, tiled=True)

    s = jnp.arange(total, dtype=jnp.int32)
    s_row = s // (local_rows * n_col)
    s_col = (s // local_rows) % n_col
    s_off = s % local_rows
    pos_of_stored = s_col * (n_row * local_rows) + s_row * local_rows + s_off
    inv = jnp.zeros((total,), jnp.int32).at[layout].set(s)

    def row_of(p):
        g = p // block
        core = g % n_core
        xh = (g // n_core) % n_xh
        z = g // (n_core * n_xh)
        return ((z * n_core + core) * n_xh + xh) * block + (p % block)

    p_all = jnp.arange(total, dtype=jnp.int32)
    first = partner > p_all
    rank = jnp.cumsum(first.astype(jnp.int32)) - 1
    k = jnp.arange(total // 2, dtype=jnp.int32)
    hits = first[None, :] & (rank[None, :] == k[:, None])
    rep = jnp.sum(jnp.where(hits, p_all[None, :], 0), axis=1)
    other = partner[rep]

    ladder = jnp.dot(gathered, integrals, preferred_element_type=jnp.float32)
    difference = pair_differences(
        ladder, pos_of_stored[inv[rep]], pos_of_stored[inv[other]], row_of(rep), row_of(other)
    )
    part = lax.psum_scatter(difference, ("z", "core"), scatter_dimension=0, tiled=True)
    return sum_over_pair(part.reshape(n_xh, block, part.shape[1]))


def solution(mesh):
    n_row, n_col = mesh.devices.shape
    fine = Mesh(mesh.devices.reshape(4, n_row // 8, 2, 2, n_col // 2), ROW_AXES + COL_AXES)
    return jax.shard_map(
        per_device,
        mesh=fine,
        in_specs=(P(ROW_AXES + COL_AXES, None), P(ROW_AXES, COL_AXES), P(), P()),
        out_specs=P(ROW_AXES, COL_AXES),
        check_vma=False,
    )
```

```python
import jax
import jax.numpy as jnp
from jax import lax
from jax.experimental import pallas as pl
from jax.experimental.pallas import tpu as pltpu
from jax.sharding import Mesh, PartitionSpec as P

ROW_AXES = ("z", "xh", "core")
COL_AXES = ("xl", "y")


def _antisym_kernel(own_idx, partner_idx, all_ref, out_ref, own_buf, partner_buf, sem):
    rows = out_ref.shape[0]
    step = pl.program_id(0)
    steps = pl.num_programs(0)

    def issue(at, slot):
        base = at * rows

        def body(r, carry):
            pltpu.make_async_copy(all_ref.at[pl.ds(own_idx[base + r], 1)], own_buf.at[slot, pl.ds(r, 1)], sem.at[0, slot]).start()
            pltpu.make_async_copy(all_ref.at[pl.ds(partner_idx[base + r], 1)], partner_buf.at[slot, pl.ds(r, 1)], sem.at[1, slot]).start()
            return carry

        lax.fori_loop(0, rows, body, 0)

    @pl.when(step == 0)
    def _():
        issue(0, 0)

    @pl.when(step + 1 < steps)
    def _():
        issue(step + 1, (step + 1) % 2)

    slot = step % 2
    pltpu.make_async_copy(all_ref.at[pl.ds(0, rows)], own_buf.at[slot], sem.at[0, slot]).wait()
    pltpu.make_async_copy(all_ref.at[pl.ds(0, rows)], partner_buf.at[slot], sem.at[1, slot]).wait()
    out_ref[...] = own_buf[slot] - partner_buf[slot]


def antisymmetrize(ladder, own_rows, partner_rows, rows=128):
    total, width = ladder.shape
    return pl.pallas_call(
        _antisym_kernel,
        grid_spec=pltpu.PrefetchScalarGridSpec(
            num_scalar_prefetch=2,
            grid=(total // rows,),
            in_specs=[pl.BlockSpec(memory_space=pl.ANY)],
            out_specs=pl.BlockSpec((rows, width), lambda b, own, other: (b, 0)),
            scratch_shapes=[
                pltpu.VMEM((2, rows, width), ladder.dtype),
                pltpu.VMEM((2, rows, width), ladder.dtype),
                pltpu.SemaphoreType.DMA((2, 2)),
            ],
        ),
        out_shape=jax.ShapeDtypeStruct(ladder.shape, ladder.dtype),
        compiler_params=pltpu.CompilerParams(dimension_semantics=("arbitrary",)),
        cost_estimate=pl.CostEstimate(flops=total * width, transcendentals=0, bytes_accessed=3 * total * width * 4),
    )(own_rows, partner_rows, ladder)


def _pair_diff_kernel(a_idx, b_idx, ia_idx, ib_idx, all_ref, out_ref, a_buf, b_buf, o_buf, in_sem, out_sem):
    rows = a_buf.shape[1]
    step = pl.program_id(0)
    steps = pl.num_programs(0)

    def issue(at, slot):
        base = at * rows

        def body(r, carry):
            pltpu.make_async_copy(all_ref.at[pl.ds(a_idx[base + r], 1)], a_buf.at[slot, pl.ds(r, 1)], in_sem.at[0, slot]).start()
            pltpu.make_async_copy(all_ref.at[pl.ds(b_idx[base + r], 1)], b_buf.at[slot, pl.ds(r, 1)], in_sem.at[1, slot]).start()
            return carry

        lax.fori_loop(0, rows, body, 0)

    def drain(slot):
        pltpu.make_async_copy(o_buf.at[slot], out_ref.at[pl.ds(0, 2 * rows)], out_sem.at[slot]).wait()

    @pl.when(step == 0)
    def _():
        issue(0, 0)

    @pl.when(step + 1 < steps)
    def _():
        issue(step + 1, (step + 1) % 2)

    slot = step % 2
    pltpu.make_async_copy(all_ref.at[pl.ds(0, rows)], a_buf.at[slot], in_sem.at[0, slot]).wait()
    pltpu.make_async_copy(all_ref.at[pl.ds(0, rows)], b_buf.at[slot], in_sem.at[1, slot]).wait()

    @pl.when(step >= 2)
    def _():
        drain(slot)

    d = a_buf[slot] - b_buf[slot]
    o_buf[slot, pl.ds(0, rows)] = d
    o_buf[slot, pl.ds(rows, rows)] = -d
    base = step * rows

    def put(r, carry):
        pltpu.make_async_copy(o_buf.at[slot, pl.ds(r, 1)], out_ref.at[pl.ds(ia_idx[base + r], 1)], out_sem.at[slot]).start()
        pltpu.make_async_copy(o_buf.at[slot, pl.ds(rows + r, 1)], out_ref.at[pl.ds(ib_idx[base + r], 1)], out_sem.at[slot]).start()
        return carry

    lax.fori_loop(0, rows, put, 0)

    @pl.when(step == steps - 1)
    def _():
        drain(slot)

        @pl.when(steps >= 2)
        def _():
            drain(1 - slot)


def pair_differences(ladder, a_rows, b_rows, a_out, b_out, rows=64):
    total, width = ladder.shape
    pairs = a_rows.shape[0]
    return pl.pallas_call(
        _pair_diff_kernel,
        grid_spec=pltpu.PrefetchScalarGridSpec(
            num_scalar_prefetch=4,
            grid=(pairs // rows,),
            in_specs=[pl.BlockSpec(memory_space=pl.ANY)],
            out_specs=pl.BlockSpec(memory_space=pl.ANY),
            scratch_shapes=[
                pltpu.VMEM((2, rows, width), ladder.dtype),
                pltpu.VMEM((2, rows, width), ladder.dtype),
                pltpu.VMEM((2, 2 * rows, width), ladder.dtype),
                pltpu.SemaphoreType.DMA((2, 2)),
                pltpu.SemaphoreType.DMA((2,)),
            ],
        ),
        out_shape=jax.ShapeDtypeStruct(ladder.shape, ladder.dtype),
        compiler_params=pltpu.CompilerParams(dimension_semantics=("arbitrary",)),
        cost_estimate=pl.CostEstimate(flops=total * width, transcendentals=0, bytes_accessed=2 * total * width * 4),
    )(a_rows, b_rows, a_out, b_out, ladder)


def _exchange_kernel(src_ref, out_ref, send_sem, recv_sem, local_sem):
    n_z, n_xh, n_core = (lax.axis_size(a) for a in ROW_AXES)
    n = n_z * n_xh * n_core
    z, xh, core, xl, y = (lax.axis_index(a) for a in ROW_AXES + COL_AXES)
    me = (z * n_xh + xh) * n_core + core

    def peer(k):
        t = lax.rem(me + k, n)
        return t, (t // (n_xh * n_core), lax.rem(t // n_core, n_xh), lax.rem(t, n_core), xl, y)

    local = pltpu.make_async_copy(src_ref.at[me], out_ref.at[me], local_sem.at[0])
    local.start()
    sends = []
    for k in range(1, n):
        t, where = peer(k)
        copy = pltpu.make_async_remote_copy(
            src_ref=src_ref.at[t],
            dst_ref=out_ref.at[me],
            send_sem=send_sem.at[k - 1],
            recv_sem=recv_sem.at[0],
            device_id=where,
            device_id_type=pl.DeviceIdType.MESH,
        )
        copy.start()
        sends.append(copy)
    for copy in sends:
        copy.wait_send()
    pltpu.make_async_copy(src_ref.at[pl.ds(0, n - 1)], out_ref.at[pl.ds(0, n - 1)], recv_sem.at[0]).wait()
    local.wait()


def exchange_over_row(pieces):
    n = pieces.shape[0]
    return pl.pallas_call(
        _exchange_kernel,
        out_shape=jax.ShapeDtypeStruct(pieces.shape, pieces.dtype),
        in_specs=[pl.BlockSpec(memory_space=pl.ANY)],
        out_specs=pl.BlockSpec(memory_space=pl.ANY),
        scratch_shapes=[
            pltpu.SemaphoreType.DMA((n - 1,)),
            pltpu.SemaphoreType.DMA((1,)),
            pltpu.SemaphoreType.DMA((1,)),
        ],
        compiler_params=pltpu.CompilerParams(has_side_effects=True),
    )(pieces)


def _pair_sum_kernel(part_ref, out_ref, own_buf, recv_buf, send_sem, recv_sem, local_sem):
    n_xh = lax.axis_size("xh")
    z, xh, core, xl, y = (lax.axis_index(a) for a in ROW_AXES + COL_AXES)
    other = lax.rem(xh + 1, n_xh)
    where = (z, other, core, xl, y)
    pieces = send_sem.shape[0]
    rows = own_buf.shape[0] // pieces

    barrier = pltpu.get_barrier_semaphore()
    pl.semaphore_signal(barrier, inc=1, device_id=where, device_id_type=pl.DeviceIdType.MESH)
    pl.semaphore_wait(barrier, 1)

    local = pltpu.make_async_copy(part_ref.at[xh], own_buf, local_sem.at[0])
    local.start()
    sends = []
    for k in range(pieces):
        copy = pltpu.make_async_remote_copy(
            src_ref=part_ref.at[other, pl.ds(k * rows, rows)],
            dst_ref=recv_buf.at[pl.ds(k * rows, rows)],
            send_sem=send_sem.at[k],
            recv_sem=recv_sem.at[0],
            device_id=where,
            device_id_type=pl.DeviceIdType.MESH,
        )
        copy.start()
        sends.append(copy)
    local.wait()
    for copy in sends:
        copy.wait_send()
    pltpu.make_async_copy(part_ref.at[xh], recv_buf, recv_sem.at[0]).wait()
    out_ref[...] = (own_buf[...] + recv_buf[...]).astype(out_ref.dtype)


def sum_over_pair(part, pieces=4):
    _, rows, width = part.shape
    return pl.pallas_call(
        _pair_sum_kernel,
        out_shape=jax.ShapeDtypeStruct((rows, width), jnp.bfloat16),
        in_specs=[pl.BlockSpec(memory_space=pl.ANY)],
        out_specs=pl.BlockSpec(memory_space=pltpu.VMEM),
        scratch_shapes=[
            pltpu.VMEM((rows, width), part.dtype),
            pltpu.VMEM((rows, width), part.dtype),
            pltpu.SemaphoreType.DMA((pieces,)),
            pltpu.SemaphoreType.DMA((1,)),
            pltpu.SemaphoreType.DMA((1,)),
        ],
        compiler_params=pltpu.CompilerParams(collective_id=1, has_side_effects=True),
    )(part)


def per_device(stored, integrals, layout, partner):
    local_rows = stored.shape[0]
    n_z = lax.axis_size("z")
    n_xh = lax.axis_size("xh")
    n_core = lax.axis_size("core")
    n_row = n_z * n_xh * n_core
    n_col = lax.axis_size(COL_AXES)
    total = local_rows * n_row * n_col
    block = total // n_row

    pieces = stored.reshape(local_rows, n_row, stored.shape[1] // n_row).transpose(1, 0, 2)
    regrouped = exchange_over_row(pieces).reshape(n_row * local_rows, pieces.shape[2])
    gathered = lax.all_gather(regrouped, COL_AXES, axis=0, tiled=True)

    s = jnp.arange(total, dtype=jnp.int32)
    s_row = s // (local_rows * n_col)
    s_col = (s // local_rows) % n_col
    s_off = s % local_rows
    pos_of_stored = s_col * (n_row * local_rows) + s_row * local_rows + s_off
    inv = jnp.zeros((total,), jnp.int32).at[layout].set(s)

    def row_of(p):
        g = p // block
        core = g % n_core
        xh = (g // n_core) % n_xh
        z = g // (n_core * n_xh)
        return ((z * n_core + core) * n_xh + xh) * block + (p % block)

    p_all = jnp.arange(total, dtype=jnp.int32)
    first = partner > p_all
    rank = jnp.cumsum(first.astype(jnp.int32)) - 1
    k = jnp.arange(total // 2, dtype=jnp.int32)
    hits = first[None, :] & (rank[None, :] == k[:, None])
    rep = jnp.sum(jnp.where(hits, p_all[None, :], 0), axis=1)
    other = partner[rep]

    ladder = jnp.dot(gathered, integrals, preferred_element_type=jnp.float32)
    difference = pair_differences(
        ladder, pos_of_stored[inv[rep]], pos_of_stored[inv[other]], row_of(rep), row_of(other)
    )
    part = lax.psum_scatter(difference, ("z", "core"), scatter_dimension=0, tiled=True)
    return sum_over_pair(part.reshape(n_xh, block, part.shape[1]))


def solution(mesh):
    n_row, n_col = mesh.devices.shape
    fine = Mesh(mesh.devices.reshape(4, n_row // 8, 2, 2, n_col // 2), ROW_AXES + COL_AXES)
    return jax.shard_map(
        per_device,
        mesh=fine,
        in_specs=(P(ROW_AXES + COL_AXES, None), P(ROW_AXES, COL_AXES), P(), P()),
        out_specs=P(ROW_AXES, COL_AXES),
        check_vma=False,
    )
```
